512 devices in a mesh: walk: 8 (over x, core), param: 64 (over z, y).
Axes of the slice: x: 4, y: 4, z: 16, core: 2. Of those that a mesh axis runs over, the one named last changes fastest.
Arguments:
- jacobian: float32 [1024, 606208], P('walk', 'param'), may hold values from -0.16722973 to 0.16722973, as said below
- energies: float32 [1024], P('walk'), may hold values from -6 to 6
- shifts: float32 [8], replicated, may hold values from 1.6495989e-06 to 4.9487964e-05
Outputs:
- update: float32 [8, 606208], P(None, 'param')
The draws below stay inside these ranges and needn't reach their ends.
Inputs may be any that keep to these rules, and one draw needn't show every extreme that they name: `jacobian`: Real-valued entries of both signs.
All inputs are finite; a program needn't handle non-finite values.
Results may differ from the reference program's by a relative error of at most 0.00028.
Values sent between devices are 32-bit elements; how exact they have to be, the bound alone decides.
A program may use at most 64 MiB of HBM per device.

```python
import math
import jax
import jax.numpy as jnp
from jax import lax

SHIFTS = 8
ITERS = 3
WALKERS = 1024
PARAMS = 606208


def draw_jacobian(key, part):
    key_noise, key_rows, key_cols, key_offset = jax.random.split(key, 4)
    walk_pos = jnp.arange(WALKERS, dtype=jnp.float32) / WALKERS
    param_pos = jnp.arange(PARAMS, dtype=jnp.float32) / PARAMS
    base_scale = jnp.sqrt(jnp.float32(WALKERS)) / (20.0 * PARAMS)
    col_offset = jax.random.truncated_normal(key_offset, -4.0, 4.0, (PARAMS,), jnp.float32)
    ramp_log = jnp.log(3.0)
    noise_draw = jax.random.truncated_normal(key_noise, -4.0, 4.0, (WALKERS, PARAMS), jnp.float32)
    row_scale = jnp.exp(jax.random.uniform(key_rows, (WALKERS,), jnp.float32) * jnp.log(10.0) + ramp_log * walk_pos)
    col_scale = jnp.exp(jax.random.uniform(key_cols, (PARAMS,), jnp.float32) * jnp.log(10.0) + ramp_log * param_pos)
    inner = row_scale[:, None] * noise_draw + col_offset[None, :]
    return (base_scale * col_scale[None, :] * inner).astype(jnp.float32)


def block_scale(stream_key, extent, cuts, low, high):
    loudness, own = 1.0, jax.random.fold_in(stream_key, 6)
    for dim, shards_of in cuts:
        draws = jnp.exp(jax.random.uniform(jax.random.fold_in(own, dim), (shards_of,), jnp.float32, low / len(cuts), high / len(cuts)))
        loudness = loudness * jnp.repeat(draws, extent[dim] // shards_of).reshape([-1 if axis == dim else 1 for axis in range(len(extent))])
    return loudness


def scatter_about(stream_key, extent, width, reach, shards=(), kind=jnp.bfloat16):
    entries = width * jax.random.normal(stream_key, extent, jnp.float32)
    if shards:
        entries = entries * block_scale(stream_key, extent, shards, -0.22, 0.18)
    return jnp.clip(entries, -reach, reach).astype(kind)


def setup_inputs(seed: int = 0) -> dict:
    splits = jax.random.split(jax.random.key(seed), 4)
    return {
        "jacobian": draw_jacobian(jax.random.fold_in(splits[3], 71), 0),
        "energies": scatter_about(splits[1], (WALKERS,), 1.0, 6.0, ((0, 8),), jnp.float32),
        "shifts": jnp.clip(jnp.exp(jax.random.uniform(splits[2], (SHIFTS,), jnp.float32, math.log(1.6495988575115916e-06), math.log(4.948796413373202e-05))), 1.6495988575115916e-06, 4.948796413373202e-05),
    }


highest = lax.Precision.HIGHEST

def reference(jacobian, energies, shifts):
    walkers = jacobian.shape[0]
    column_mean = lax.optimization_barrier(jnp.sum(jacobian, axis=0)) / walkers
    energy_dev = energies - jnp.sum(energies) / walkers
    gradient = (jnp.dot(energy_dev, jacobian, precision=highest) - column_mean * jnp.sum(energy_dev)) / walkers

    def operate(direction):
        projected = lax.dot_general(direction, jacobian, (((1,), (1,)), ((), ())), precision=highest)
        projected = projected - jnp.dot(direction, column_mean, precision=highest)[:, None]
        back_terms = jnp.dot(projected, jacobian, precision=highest)
        return back_terms / walkers + shifts[:, None] * direction
    residual = jnp.broadcast_to(gradient[None, :], (shifts.shape[0], jacobian.shape[1]))
    direction = residual
    solution = jnp.zeros_like(residual)
    norm_now = lax.optimization_barrier(jnp.sum(residual * residual, axis=1))
    for number in range(ITERS):
        applied = operate(direction)
        step_size = norm_now / lax.optimization_barrier(jnp.sum(direction * applied, axis=1))
        solution = solution + step_size[:, None] * direction
        residual = residual - step_size[:, None] * applied
        norm_next = lax.optimization_barrier(jnp.sum(residual * residual, axis=1))
        direction = residual + (norm_next / norm_now)[:, None] * direction
        norm_now = norm_next
    norm_scale = lax.rsqrt(lax.optimization_barrier(jnp.mean(solution * solution, axis=1)) + 1e-06)
    return solution * norm_scale[:, None]
```

```python
import functools

import jax
import jax.numpy as jnp
from jax import lax
from jax.experimental import pallas as pl
from jax.experimental.pallas import tpu as pltpu
from jax.sharding import PartitionSpec as P

EPSILON = 1e-06
LANE = 128
Y_SIZE = 4
MESH = pl.DeviceIdType.MESH


def lane_pick(row, lane, number):
    return jnp.sum(jnp.where(lane == number, row, 0.0), axis=1, keepdims=True)


def lane_pack(lane, values):
    row = jnp.zeros(lane.shape, jnp.float32)
    for number, value in enumerate(values):
        row = jnp.where(lane == number, value, row)
    return row


def dot_row(left, right):
    return jnp.sum(left * right, axis=1, keepdims=True)


def as_column(row):
    return jnp.transpose(jnp.broadcast_to(row, (LANE, LANE)))


def kernel(
    dims,
    jac_hbm, energy_ref, shift_ref, out_ref,
    jac, part0, part, got0, got, base, next1, next2,
    ybuf, zbuf, last, load_sem, walk_send, walk_recv, param_send, param_recv,
):
    nw, ny, nz, cols, blocks = dims
    width = blocks * LANE
    walkers = float(nw * LANE)
    params = float(ny * nz * cols)
    w = lax.axis_index("walk")
    p = lax.axis_index("param")
    y, z = lax.rem(p, ny), p // ny

    load = pltpu.make_async_copy(jac_hbm, jac.at[:, pl.ds(0, cols)], load_sem)
    load.start()

    barrier = pltpu.get_barrier_semaphore()

    def walk_peer(d):
        return (lax.rem(w + d, nw), p)

    def y_peer(d):
        return (w, z * ny + lax.rem(y + d, ny))

    def z_peer(d):
        return (w, lax.rem(z + d, nz) * ny + y)

    def each(count, step):
        def go(d, carry):
            step(d)
            return carry
        lax.fori_loop(1, count, go, 0)

    for count, peer in ((nw, walk_peer), (ny, y_peer), (nz, z_peer)):
        each(count, lambda d, peer=peer: pl.semaphore_signal(
            barrier, inc=1, device_id=peer(d), device_id_type=MESH))

    if nw * width > cols:
        jac[:, cols:] = jnp.zeros((LANE, nw * width - cols), jnp.float32)

    lane = lax.broadcasted_iota(jnp.int32, (1, LANE), 1)
    energy = energy_ref[...]
    group_mean = jnp.sum(energy, axis=1, keepdims=True) / float(LANE)
    energy_col = as_column(energy - group_mean)
    mean_row = jnp.broadcast_to(group_mean, (1, LANE))
    load.wait()

    def first_pass(k, carry):
        for b in range(blocks):
            block = jac[:, pl.ds(pl.multiple_of(k * width + b * LANE, LANE), LANE)]
            part0[k, :, b * LANE:(b + 1) * LANE] = jnp.sum(block * energy_col, axis=0, keepdims=True)
            part0[k, :, width + b * LANE:width + (b + 1) * LANE] = jnp.sum(block, axis=0, keepdims=True)
        part0[k, :, 2 * width:] = mean_row
        return carry
    lax.fori_loop(0, nw, first_pass, 0)

    pl.semaphore_wait(barrier, (nw - 1) + (ny - 1) + (nz - 1))

    def exchange(count, source, target, landed, send, recv, peer):
        def copy(d, dst):
            return pltpu.make_async_remote_copy(
                src_ref=source(d), dst_ref=dst, send_sem=send.at[d], recv_sem=recv.at[d],
                device_id=peer(d), device_id_type=MESH)
        each(count, lambda d: copy(d, target(d)).start())
        each(count, lambda d: copy(d, landed(d)).wait_recv())
        each(count, lambda d: copy(d, target(d)).wait_send())

    def scatter(number, pieces, buffer):
        exchange(nw, lambda d: pieces.at[lax.rem(w + d, nw)], lambda d: buffer.at[d], lambda d: buffer.at[d],
                 walk_send, walk_recv.at[number], walk_peer)

    def gather(number, buffer):
        exchange(nw, lambda d: buffer.at[w], lambda d: buffer.at[w], lambda d: buffer.at[lax.rem(w + nw - d, nw)],
                 walk_send, walk_recv.at[number], walk_peer)

    def param_sum(number, row):
        ys, zs = ybuf.at[number], zbuf.at[number]
        ys[0] = row
        exchange(ny, lambda d: ys.at[0], lambda d: ys.at[d], lambda d: ys.at[d],
                 param_send, param_recv.at[2 * number], y_peer)
        zs[0] = jnp.sum(ys[...], axis=0)
        exchange(nz, lambda d: zs.at[0], lambda d: zs.at[d], lambda d: zs.at[d],
                 param_send, param_recv.at[2 * number + 1], z_peer)
        return jnp.sum(zs[...], axis=0)

    scatter(0, part0, got0)
    own = part0[w]
    mean_total = own[:, 2 * width:]
    for d in range(1, nw):
        mean_total = mean_total + got0[d, :, 2 * width:]
    energy_mean = mean_total[:, :1] / float(nw)
    delta = own[:, 2 * width:2 * width + 1] - energy_mean
    column_sum = own[:, width:2 * width]
    force = own[:, :width] + delta * own[:, width:2 * width]
    dev_sum = delta
    for d in range(1, nw):
        delta = got0[d, :, 2 * width:2 * width + 1] - energy_mean
        piece = got0[d, :, width:2 * width]
        column_sum = column_sum + piece
        force = force + got0[d, :, :width] + delta * piece
        dev_sum = dev_sum + delta
    column_mean = column_sum / walkers
    base[w, :, :width] = (force - column_mean * (dev_sum * float(LANE))) / walkers
    base[w, :, width:] = column_mean
    gather(1, base)

    def project(vector, others):
        def step(k, carry):
            total, centre, dots = carry
            for b in range(blocks):
                row = vector[k, :, b * LANE:(b + 1) * LANE]
                block = jac[:, pl.ds(pl.multiple_of(k * width + b * LANE, LANE), LANE)]
                total = total + block * row
                centre = centre + base[k, :, width + b * LANE:width + (b + 1) * LANE] * row
                dots = tuple(
                    dot + other[k, :, b * LANE:(b + 1) * LANE] * row
                    for dot, other in zip(dots, others))
            return total, centre, dots
        zero = jnp.zeros((1, LANE), jnp.float32)
        total, centre, dots = lax.fori_loop(
            0, nw, step, (jnp.zeros((LANE, LANE), jnp.float32), zero, (zero,) * len(others)))
        row = jnp.sum(jnp.transpose(total), axis=0, keepdims=True)
        centre = jnp.sum(centre, axis=1, keepdims=True)
        dots = [jnp.sum(dot, axis=1, keepdims=True) for dot in dots]
        return jnp.concatenate([row - centre, lane_pack(lane, dots)], axis=1)

    def spread(weights, scalars):
        column = as_column(weights)

        def step(k, carry):
            for b in range(blocks):
                block = jac[:, pl.ds(pl.multiple_of(k * width + b * LANE, LANE), LANE)]
                part[k, :, b * LANE:(b + 1) * LANE] = jnp.sum(block * column, axis=0, keepdims=True)
            part[k, :, width:] = scalars
            return carry
        lax.fori_loop(0, nw, step, 0)

    def collect():
        total = part[w]
        for d in range(1, nw):
            total = total + got[d]
        return total[:, :width] / walkers, total[:, width:]

    seed_shift = shift_ref[0]

    reply = param_sum(0, project(base, (base,)))
    q0, m00 = reply[:, :LANE], lane_pick(reply[:, LANE:], lane, 0)
    spread(q0, lane_pack(lane, [dot_row(q0, q0)]))
    scatter(2, part, got)
    image, sums = collect()
    k00 = lane_pick(sums, lane, 0) / walkers
    r0 = base[w, :, :width]
    r1 = r0 - (m00 / (k00 + seed_shift * m00)) * (image + seed_shift * r0)
    next1[w] = r1
    gather(3, next1)

    reply = param_sum(1, project(next1, (next1, base)))
    q1, sums = reply[:, :LANE], reply[:, LANE:]
    m11, m01 = lane_pick(sums, lane, 0), lane_pick(sums, lane, 1)
    turn = m11 / m00
    p1 = q1 + turn * q0
    spread(p1, lane_pack(lane, [dot_row(q1, q1), dot_row(q0, q1), dot_row(p1, p1)]))
    scatter(4, part, got)
    image, sums = collect()
    k11, k01, pp1 = (lane_pick(sums, lane, i) / walkers for i in range(3))
    d1 = r1 + turn * r0
    dd1 = m11 + 2.0 * turn * m01 + turn * turn * m00
    next2[w] = r1 - (m11 / (pp1 + seed_shift * dd1)) * (image + seed_shift * d1)
    gather(5, next2)

    reply = param_sum(2, project(next2, (next2, base, next1)))
    q2, sums = reply[:, :LANE], reply[:, LANE:]
    m22, m02, m12 = (lane_pick(sums, lane, i) for i in range(3))
    last[0] = lane_pack(lane, [dot_row(q2, q2), dot_row(q0, q2), dot_row(q1, q2)])
    exchange(nw, lambda d: last.at[0], lambda d: last.at[d], lambda d: last.at[d],
             walk_send, walk_recv.at[6], walk_peer)
    sums = jnp.sum(last[...], axis=0)
    k22, k02, k12 = (lane_pick(sums, lane, i) / walkers for i in range(3))

    count = out_ref.shape[0]
    trial = lax.broadcasted_iota(jnp.int32, (count, LANE), 0)
    shift = jnp.zeros((count, LANE), jnp.float32)
    for number in range(count):
        shift = jnp.where(trial == number, shift_ref[number], shift)
    a00, a01, a02 = k00 + shift * m00, k01 + shift * m01, k02 + shift * m02
    a11, a12, a22 = k11 + shift * m11, k12 + shift * m12, k22 + shift * m22
    l10, l20 = a01 / a00, a02 / a00
    e1 = a11 - l10 * a01
    e21 = a12 - l20 * a01
    l21 = e21 / e1
    e2 = a22 - l20 * a02 - l21 * e21
    b1 = m01 - l10 * m00
    b2 = m02 - l20 * m00 - l21 * b1
    c2 = b2 / e2
    c1 = b1 / e1 - l21 * c2
    c0 = m00 / a00 - l10 * c1 - l20 * c2
    square = c0 * (c0 * m00 + 2.0 * (c1 * m01 + c2 * m02)) + c1 * (c1 * m11 + 2.0 * c2 * m12) + c2 * c2 * m22
    scale = lax.rsqrt(square / params + EPSILON)
    c0, c1, c2 = c0 * scale, c1 * scale, c2 * scale

    def write(k, b):
        at = slice(b * LANE, (b + 1) * LANE)
        out_ref[:, pl.ds(pl.multiple_of(k * width + b * LANE, LANE), LANE)] = (
            c0 * base[k, :, at] + c1 * next1[k, :, at] + c2 * next2[k, :, at])

    whole = cols // width

    def write_piece(k, carry):
        for b in range(blocks):
            write(k, b)
        return carry
    lax.fori_loop(0, whole, write_piece, 0)
    for b in range((cols - whole * width) // LANE):
        write(whole, b)


def solution(mesh):
    nw, npar = mesh.shape["walk"], mesh.shape["param"]
    ny = Y_SIZE
    nz = npar // ny

    def body(jacobian, energies, shifts):
        cols = jacobian.shape[1]
        blocks = -(-(cols // LANE) // nw)
        width = blocks * LANE
        count = shifts.shape[0]
        f32 = jnp.float32
        return pl.pallas_call(
            functools.partial(kernel, (nw, ny, nz, cols, blocks)),
            out_shape=jax.ShapeDtypeStruct((count, cols), f32),
            in_specs=[
                pl.BlockSpec(memory_space=pl.ANY),
                pl.BlockSpec(memory_space=pltpu.VMEM),
                pl.BlockSpec(memory_space=pltpu.SMEM),
            ],
            out_specs=pl.BlockSpec(memory_space=pltpu.VMEM),
            scratch_shapes=[
                pltpu.VMEM((LANE, nw * width), f32),
                pltpu.VMEM((nw, 1, 2 * width + LANE), f32),
                pltpu.VMEM((nw, 1, width + LANE), f32),
                pltpu.VMEM((nw, 1, 2 * width + LANE), f32),
                pltpu.VMEM((nw, 1, width + LANE), f32),
                pltpu.VMEM((nw, 1, 2 * width), f32),
                pltpu.VMEM((nw, 1, width), f32),
                pltpu.VMEM((nw, 1, width), f32),
                pltpu.VMEM((3, ny, 1, 2 * LANE), f32),
                pltpu.VMEM((3, nz, 1, 2 * LANE), f32),
                pltpu.VMEM((nw, 1, LANE), f32),
                pltpu.SemaphoreType.DMA,
                pltpu.SemaphoreType.DMA((nw,)),
                pltpu.SemaphoreType.DMA((7, nw)),
                pltpu.SemaphoreType.DMA((nz,)),
                pltpu.SemaphoreType.DMA((6, nz)),
            ],
            compiler_params=pltpu.CompilerParams(
                collective_id=0, has_side_effects=True, vmem_limit_bytes=48 << 20
            ),
        )(jacobian, energies.reshape(1, -1), shifts)

    return jax.shard_map(
        body,
        mesh=mesh,
        in_specs=(P("walk", "param"), P("walk"), P()),
        out_specs=P(None, "param"),
        check_vma=False,
    )
```

```python
import functools

import jax
import jax.numpy as jnp
from jax import lax
from jax.experimental import pallas as pl
from jax.experimental.pallas import tpu as pltpu
from jax.sharding import PartitionSpec as P

EPSILON = 1e-06
LANE = 128
Y_SIZE = 4
MESH = pl.DeviceIdType.MESH


def lane_pick(row, lane, number):
    return jnp.sum(jnp.where(lane == number, row, 0.0), axis=1, keepdims=True)


def lane_pack(lane, values):
    row = jnp.zeros(lane.shape, jnp.float32)
    for number, value in enumerate(values):
        row = jnp.where(lane == number, value, row)
    return row


def dot_row(left, right):
    return jnp.sum(left * right, axis=1, keepdims=True)


def as_column(row):
    return jnp.transpose(jnp.broadcast_to(row, (LANE, LANE)))


def kernel(
    dims,
    jac_hbm, energy_hbm, shift_hbm, out_ref,
    jac, energy_ref, shift_ref, part0, got0, base, next1, next2, full, sums_buf,
    ybuf, zbuf, load_sem, walk_send, walk_recv, full_send, full_recv, small_send, small_recv,
    param_send, param_recv,
):
    nw, ny, nz, cols, blocks = dims
    width = blocks * LANE
    walkers = float(nw * LANE)
    params = float(ny * nz * cols)
    w = lax.axis_index("walk")
    p = lax.axis_index("param")
    y, z = lax.rem(p, ny), p // ny

    load = pltpu.make_async_copy(jac_hbm, jac.at[:, pl.ds(0, cols)], load_sem.at[0])
    load_energy = pltpu.make_async_copy(energy_hbm, energy_ref, load_sem.at[1])
    load_shift = pltpu.make_async_copy(shift_hbm, shift_ref, load_sem.at[2])
    load_energy.start()
    load_shift.start()
    load.start()

    barrier = pltpu.get_barrier_semaphore()

    def walk_peer(d):
        return (lax.rem(w + d, nw), p)

    def y_peer(d):
        return (w, z * ny + lax.rem(y + d, ny))

    def z_peer(d):
        return (w, lax.rem(z + d, nz) * ny + y)

    def each(count, step):
        def go(d, carry):
            step(d)
            return carry
        lax.fori_loop(1, count, go, 0)

    for count, peer in ((nw, walk_peer), (ny, y_peer), (nz, z_peer)):
        each(count, lambda d, peer=peer: pl.semaphore_signal(
            barrier, inc=1, device_id=peer(d), device_id_type=MESH))

    if nw * width > cols:
        jac[:, cols:] = jnp.zeros((LANE, nw * width - cols), jnp.float32)

    lane = lax.broadcasted_iota(jnp.int32, (1, LANE), 1)
    load_energy.wait()
    load_shift.wait()
    energy = energy_ref[...]
    group_mean = jnp.sum(energy, axis=1, keepdims=True) / float(LANE)
    energy_col = as_column(energy - group_mean)
    mean_row = jnp.broadcast_to(group_mean, (1, LANE))
    load.wait()

    def first_pass(k, carry):
        for b in range(blocks):
            block = jac[:, pl.ds(pl.multiple_of(k * width + b * LANE, LANE), LANE)]
            part0[k, :, b * LANE:(b + 1) * LANE] = jnp.sum(block * energy_col, axis=0, keepdims=True)
            part0[k, :, width + b * LANE:width + (b + 1) * LANE] = jnp.sum(block, axis=0, keepdims=True)
        part0[k, :, 2 * width:] = mean_row
        return carry
    lax.fori_loop(0, nw, first_pass, 0)

    pl.semaphore_wait(barrier, (nw - 1) + (ny - 1) + (nz - 1))

    def exchange(count, source, target, landed, send, recv, peer):
        def copy(d, dst):
            return pltpu.make_async_remote_copy(
                src_ref=source(d), dst_ref=dst, send_sem=send.at[d], recv_sem=recv.at[d],
                device_id=peer(d), device_id_type=MESH)
        each(count, lambda d: copy(d, target(d)).start())
        each(count, lambda d: copy(d, landed(d)).wait_recv())
        each(count, lambda d: copy(d, target(d)).wait_send())

    def scatter(number, pieces, buffer):
        exchange(nw, lambda d: pieces.at[lax.rem(w + d, nw)], lambda d: buffer.at[d], lambda d: buffer.at[d],
                 walk_send, walk_recv.at[number], walk_peer)

    def param_sum(number, row):
        ys, zs = ybuf.at[number], zbuf.at[number]
        ys[0] = row
        exchange(ny, lambda d: ys.at[0], lambda d: ys.at[d], lambda d: ys.at[d],
                 param_send, param_recv.at[2 * number], y_peer)
        zs[0] = jnp.sum(ys[...], axis=0)
        exchange(nz, lambda d: zs.at[0], lambda d: zs.at[d], lambda d: zs.at[d],
                 param_send, param_recv.at[2 * number + 1], z_peer)
        return jnp.sum(zs[...], axis=0)

    scatter(0, part0, got0)
    own = part0[w]
    mean_total = own[:, 2 * width:]
    for d in range(1, nw):
        mean_total = mean_total + got0[d, :, 2 * width:]
    energy_mean = mean_total[:, :1] / float(nw)
    delta = own[:, 2 * width:2 * width + 1] - energy_mean
    column_sum = own[:, width:2 * width]
    force = own[:, :width] + delta * own[:, width:2 * width]
    dev_sum = delta
    for d in range(1, nw):
        delta = got0[d, :, 2 * width:2 * width + 1] - energy_mean
        piece = got0[d, :, width:2 * width]
        column_sum = column_sum + piece
        force = force + got0[d, :, :width] + delta * piece
        dev_sum = dev_sum + delta
    column_mean = column_sum / walkers
    base[w, :, :width] = (force - column_mean * (dev_sum * float(LANE))) / walkers
    base[w, :, width:] = column_mean

    zero_row = jnp.zeros((1, LANE), jnp.float32)

    def fresh(count):
        return jnp.zeros((LANE, LANE), jnp.float32), zero_row, (zero_row,) * count

    def project(k, carry, vector, others):
        total, centre, dots = carry
        for b in range(blocks):
            at = slice(b * LANE, (b + 1) * LANE)
            row = vector[k, :, at]
            block = jac[:, pl.ds(pl.multiple_of(k * width + b * LANE, LANE), LANE)]
            total = total + block * row
            centre = centre + base[k, :, width + b * LANE:width + (b + 1) * LANE] * row
            dots = tuple(dot + other[k, :, at] * row for dot, other in zip(dots, others))
        return total, centre, dots

    def message(carry):
        total, centre, dots = carry
        row = jnp.sum(jnp.transpose(total), axis=0, keepdims=True)
        centre = jnp.sum(centre, axis=1, keepdims=True)
        dots = [jnp.sum(dot, axis=1, keepdims=True) for dot in dots]
        return jnp.concatenate([row - centre, lane_pack(lane, dots)], axis=1)

    def spread(number, weights, scalars):
        column = as_column(weights)
        small, large = sums_buf.at[number], full.at[number]
        small[0] = lane_pack(lane, scalars)

        def small_copy(d):
            return pltpu.make_async_remote_copy(
                src_ref=small.at[0], dst_ref=small.at[d], send_sem=small_send.at[number],
                recv_sem=small_recv.at[number], device_id=walk_peer(d), device_id_type=MESH)
        each(nw, lambda d: small_copy(d).start())

        def step(k, carry):
            for b in range(blocks):
                block = jac[:, pl.ds(pl.multiple_of(k * width + b * LANE, LANE), LANE)]
                large[k, 0, :, b * LANE:(b + 1) * LANE] = jnp.sum(block * column, axis=0, keepdims=True)
            each(nw, lambda d: pltpu.make_async_remote_copy(
                src_ref=large.at[k, 0], dst_ref=large.at[k, d], send_sem=full_send.at[number, k],
                recv_sem=full_recv.at[number, k], device_id=walk_peer(d), device_id_type=MESH).start())
            return carry
        lax.fori_loop(0, nw, step, 0)

    def all_of(buffer, send, recv):
        rest = buffer.at[pl.ds(1, nw - 1)]
        return pltpu.make_async_remote_copy(
            src_ref=rest, dst_ref=rest, send_sem=send, recv_sem=recv,
            device_id=walk_peer(1), device_id_type=MESH)

    def walk_sums(number):
        whole = all_of(sums_buf.at[number], small_send.at[number], small_recv.at[number])
        whole.wait_recv()
        whole.wait_send()
        return jnp.sum(sums_buf[number], axis=0)

    def absorb(number, vector, advance, others):
        def step(k, carry):
            all_of(full.at[number, k], full_send.at[number, k], full_recv.at[number, k]).wait_recv()
            image = jnp.sum(full[number, k], axis=0) / walkers
            vector[k] = advance(k, image)
            return project(k, carry, vector, others)
        carry = lax.fori_loop(0, nw, step, fresh(len(others)))
        for k in range(nw):
            all_of(full.at[number, k], full_send.at[number, k], full_recv.at[number, k]).wait_send()
        return message(carry)

    seed_shift = shift_ref[0]

    def gather_copy(d, dst):
        return pltpu.make_async_remote_copy(
            src_ref=base.at[w], dst_ref=dst, send_sem=walk_send.at[d], recv_sem=walk_recv.at[1, d],
            device_id=walk_peer(d), device_id_type=MESH)
    each(nw, lambda d: gather_copy(d, base.at[w]).start())

    def first_step(d, carry):
        k = lax.rem(w + nw - d, nw)
        gather_copy(d, base.at[k]).wait_recv()
        return project(k, carry, base, (base,))
    carry = lax.fori_loop(1, nw, first_step, project(w, fresh(1), base, (base,)))
    each(nw, lambda d: gather_copy(d, base.at[w]).wait_send())

    reply = param_sum(0, message(carry))
    q0, m00 = reply[:, :LANE], lane_pick(reply[:, LANE:], lane, 0)
    spread(0, q0, [dot_row(q0, q0)])
    k00 = lane_pick(walk_sums(0), lane, 0) / walkers
    step0 = m00 / (k00 + seed_shift * m00)

    def advance0(k, image):
        r0 = base[k, :, :width]
        return r0 - step0 * (image + seed_shift * r0)

    reply = param_sum(1, absorb(0, next1, advance0, (next1, base)))
    q1, sums = reply[:, :LANE], reply[:, LANE:]
    m11, m01 = lane_pick(sums, lane, 0), lane_pick(sums, lane, 1)
    turn = m11 / m00
    p1 = q1 + turn * q0
    spread(1, p1, [dot_row(q1, q1), dot_row(q0, q1), dot_row(p1, p1)])
    sums = walk_sums(1)
    k11, k01, pp1 = (lane_pick(sums, lane, i) / walkers for i in range(3))
    dd1 = m11 + 2.0 * turn * m01 + turn * turn * m00
    step1 = m11 / (pp1 + seed_shift * dd1)

    def advance1(k, image):
        r1 = next1[k]
        return r1 - step1 * (image + seed_shift * (r1 + turn * base[k, :, :width]))

    reply = param_sum(2, absorb(1, next2, advance1, (next2, base, next1)))
    q2, sums = reply[:, :LANE], reply[:, LANE:]
    m22, m02, m12 = (lane_pick(sums, lane, i) for i in range(3))
    small = sums_buf.at[2]
    small[0] = lane_pack(lane, [dot_row(q2, q2), dot_row(q0, q2), dot_row(q1, q2)])
    each(nw, lambda d: pltpu.make_async_remote_copy(
        src_ref=small.at[0], dst_ref=small.at[d], send_sem=small_send.at[2],
        recv_sem=small_recv.at[2], device_id=walk_peer(d), device_id_type=MESH).start())
    sums = walk_sums(2)
    k22, k02, k12 = (lane_pick(sums, lane, i) / walkers for i in range(3))

    count = out_ref.shape[0]
    trial = lax.broadcasted_iota(jnp.int32, (count, LANE), 0)
    shift = jnp.zeros((count, LANE), jnp.float32)
    for number in range(count):
        shift = jnp.where(trial == number, shift_ref[number], shift)
    a00, a01, a02 = k00 + shift * m00, k01 + shift * m01, k02 + shift * m02
    a11, a12, a22 = k11 + shift * m11, k12 + shift * m12, k22 + shift * m22
    l10, l20 = a01 / a00, a02 / a00
    e1 = a11 - l10 * a01
    e21 = a12 - l20 * a01
    l21 = e21 / e1
    e2 = a22 - l20 * a02 - l21 * e21
    b1 = m01 - l10 * m00
    b2 = m02 - l20 * m00 - l21 * b1
    c2 = b2 / e2
    c1 = b1 / e1 - l21 * c2
    c0 = m00 / a00 - l10 * c1 - l20 * c2
    square = c0 * (c0 * m00 + 2.0 * (c1 * m01 + c2 * m02)) + c1 * (c1 * m11 + 2.0 * c2 * m12) + c2 * c2 * m22
    scale = lax.rsqrt(square / params + EPSILON)
    c0, c1, c2 = c0 * scale, c1 * scale, c2 * scale

    def write(k, b):
        at = slice(b * LANE, (b + 1) * LANE)
        out_ref[:, pl.ds(pl.multiple_of(k * width + b * LANE, LANE), LANE)] = (
            c0 * base[k, :, at] + c1 * next1[k, :, at] + c2 * next2[k, :, at])

    whole = cols // width

    def write_piece(k, carry):
        for b in range(blocks):
            write(k, b)
        return carry
    lax.fori_loop(0, whole, write_piece, 0)
    for b in range((cols - whole * width) // LANE):
        write(whole, b)


def solution(mesh):
    nw, npar = mesh.shape["walk"], mesh.shape["param"]
    ny = Y_SIZE
    nz = npar // ny

    def body(jacobian, energies, shifts):
        cols = jacobian.shape[1]
        blocks = -(-(cols // LANE) // nw)
        width = blocks * LANE
        count = shifts.shape[0]
        f32 = jnp.float32
        return pl.pallas_call(
            functools.partial(kernel, (nw, ny, nz, cols, blocks)),
            out_shape=jax.ShapeDtypeStruct((count, cols), f32),
            in_specs=[
                pl.BlockSpec(memory_space=pl.ANY),
                pl.BlockSpec(memory_space=pl.ANY),
                pl.BlockSpec(memory_space=pl.ANY),
            ],
            out_specs=pl.BlockSpec(memory_space=pltpu.VMEM),
            scratch_shapes=[
                pltpu.VMEM((LANE, nw * width), f32),
                pltpu.VMEM((1, LANE), f32),
                pltpu.SMEM((count,), f32),
                pltpu.VMEM((nw, 1, 2 * width + LANE), f32),
                pltpu.VMEM((nw, 1, 2 * width + LANE), f32),
                pltpu.VMEM((nw, 1, 2 * width), f32),
                pltpu.VMEM((nw, 1, width), f32),
                pltpu.VMEM((nw, 1, width), f32),
                pltpu.VMEM((2, nw, nw, 1, width), f32),
                pltpu.VMEM((3, nw, 1, LANE), f32),
                pltpu.VMEM((3, ny, 1, 2 * LANE), f32),
                pltpu.VMEM((3, nz, 1, 2 * LANE), f32),
                pltpu.SemaphoreType.DMA((3,)),
                pltpu.SemaphoreType.DMA((nw,)),
                pltpu.SemaphoreType.DMA((2, nw)),
                pltpu.SemaphoreType.DMA((2, nw)),
                pltpu.SemaphoreType.DMA((2, nw)),
                pltpu.SemaphoreType.DMA((3,)),
                pltpu.SemaphoreType.DMA((3,)),
                pltpu.SemaphoreType.DMA((nz,)),
                pltpu.SemaphoreType.DMA((6, nz)),
            ],
            compiler_params=pltpu.CompilerParams(
                collective_id=0, has_side_effects=True, vmem_limit_bytes=67043328
            ),
        )(jacobian, energies.reshape(1, -1), shifts)

    return jax.shard_map(
        body,
        mesh=mesh,
        in_specs=(P("walk", "param"), P("walk"), P()),
        out_specs=P(None, "param"),
        check_vma=False,
    )
```

```python
import functools

import jax
import jax.numpy as jnp
from jax import lax
from jax.experimental import pallas as pl
from jax.experimental.pallas import tpu as pltpu
from jax.sharding import PartitionSpec as P

EPSILON = 1e-06
LANE = 128
Y_SIZE = 4
MESH = pl.DeviceIdType.MESH


def lane_pick(row, lane, number):
    return jnp.sum(jnp.where(lane == number, row, 0.0), axis=1, keepdims=True)


def lane_pack(lane, values):
    row = jnp.zeros(lane.shape, jnp.float32)
    for number, value in enumerate(values):
        row = jnp.where(lane == number, value, row)
    return row


def dot_row(left, right):
    return jnp.sum(left * right, axis=1, keepdims=True)


def as_column(row):
    return jnp.transpose(jnp.broadcast_to(row, (LANE, LANE)))


def kernel(
    dims,
    jac_hbm, energy_hbm, shift_hbm, out_ref,
    jac, energy_ref, shift_ref, part0, got0, base, next1, next2, full, sums_buf,
    ybuf, zbuf, wide, load_sem, walk_send, walk_recv, full_send, full_recv, small_send, small_recv,
    param_send, param_recv,
):
    nw, ny, nz, cols, blocks = dims
    width = blocks * LANE
    walkers = float(nw * LANE)
    params = float(ny * nz * cols)
    w = lax.axis_index("walk")
    p = lax.axis_index("param")
    y, z = lax.rem(p, ny), p // ny

    load = pltpu.make_async_copy(jac_hbm, jac.at[:, pl.ds(0, cols)], load_sem.at[0])
    load_energy = pltpu.make_async_copy(energy_hbm, energy_ref, load_sem.at[1])
    load_shift = pltpu.make_async_copy(shift_hbm, shift_ref, load_sem.at[2])
    load_energy.start()
    load_shift.start()
    load.start()

    barrier = pltpu.get_barrier_semaphore()

    def walk_peer(d):
        return (lax.rem(w + d, nw), p)

    def y_peer(d):
        return (w, z * ny + lax.rem(y + d, ny))

    def z_peer(d):
        return (w, lax.rem(z + d, nz) * ny + y)

    def each(count, step):
        def go(d, carry):
            step(d)
            return carry
        lax.fori_loop(1, count, go, 0)

    for count, peer in ((nw, walk_peer), (ny, y_peer), (nz, z_peer)):
        each(count, lambda d, peer=peer: pl.semaphore_signal(
            barrier, inc=1, device_id=peer(d), device_id_type=MESH))

    if nw * width > cols:
        jac[:, cols:] = jnp.zeros((LANE, nw * width - cols), jnp.float32)

    lane = lax.broadcasted_iota(jnp.int32, (1, LANE), 1)
    load_energy.wait()
    load_shift.wait()
    energy = energy_ref[...]
    group_mean = jnp.sum(energy, axis=1, keepdims=True) / float(LANE)
    energy_col = as_column(energy - group_mean)
    mean_row = jnp.broadcast_to(group_mean, (1, LANE))
    load.wait()

    def first_pass(k, carry):
        for b in range(blocks):
            block = jac[:, pl.ds(pl.multiple_of(k * width + b * LANE, LANE), LANE)]
            part0[k, :, b * LANE:(b + 1) * LANE] = jnp.sum(block * energy_col, axis=0, keepdims=True)
            part0[k, :, width + b * LANE:width + (b + 1) * LANE] = jnp.sum(block, axis=0, keepdims=True)
        part0[k, :, 2 * width:] = mean_row
        return carry
    lax.fori_loop(0, nw, first_pass, 0)

    pl.semaphore_wait(barrier, (nw - 1) + (ny - 1) + (nz - 1))

    def exchange(count, source, target, landed, send, recv, peer):
        def copy(d, dst):
            return pltpu.make_async_remote_copy(
                src_ref=source(d), dst_ref=dst, send_sem=send.at[d], recv_sem=recv.at[d],
                device_id=peer(d), device_id_type=MESH)
        each(count, lambda d: copy(d, target(d)).start())
        each(count, lambda d: copy(d, landed(d)).wait_recv())
        each(count, lambda d: copy(d, target(d)).wait_send())

    def scatter(number, pieces, buffer):
        exchange(nw, lambda d: pieces.at[lax.rem(w + d, nw)], lambda d: buffer.at[d], lambda d: buffer.at[d],
                 walk_send, walk_recv.at[number], walk_peer)

    def far_first(count):
        return sorted(range(1, count), key=lambda d: -min(d, count - d))

    def all_of(buffer, send, recv):
        rest = buffer.at[pl.ds(1, buffer.shape[0] - 1)]
        return pltpu.make_async_remote_copy(
            src_ref=rest, dst_ref=rest, send_sem=send, recv_sem=recv,
            device_id=walk_peer(1), device_id_type=MESH)

    def spray(buffer, send, recv, count, peer):
        for d in far_first(count):
            pltpu.make_async_remote_copy(
                src_ref=buffer.at[0], dst_ref=buffer.at[d], send_sem=send, recv_sem=recv,
                device_id=peer(d), device_id_type=MESH).start()
        return all_of(buffer, send, recv)

    def direct_sum(number, row):
        mine = wide.at[number - 1]
        send, recv = param_send.at[number, 0], param_recv.at[number, 0]
        mine[0] = row

        def start(dz, dy):
            pltpu.make_async_remote_copy(
                src_ref=mine.at[0], dst_ref=mine.at[dz * ny + dy], send_sem=send, recv_sem=recv,
                device_id=(w, lax.rem(z + dz, nz) * ny + lax.rem(y + dy, ny)), device_id_type=MESH).start()

        def go(i, carry):
            dz = nz // 2 + ((i + 1) // 2) * (1 - 2 * lax.rem(i, 2))
            for dy in far_first(ny) + [0]:
                start(dz, dy)
            return carry
        lax.fori_loop(0, nz - 1, go, 0)
        for dy in far_first(ny):
            start(0, dy)
        whole = all_of(mine, send, recv)
        whole.wait_recv()
        whole.wait_send()
        return jnp.sum(mine[...], axis=0)

    def param_sum(number, row):
        ys, zs = ybuf.at[number], zbuf.at[number]
        ys[0] = row
        first = spray(ys, param_send.at[number, 0], param_recv.at[number, 0], ny, y_peer)
        first.wait_recv()
        zs[0] = jnp.sum(ys[...], axis=0)
        second = spray(zs, param_send.at[number, 1], param_recv.at[number, 1], nz, z_peer)
        first.wait_send()
        second.wait_recv()
        second.wait_send()
        return jnp.sum(zs[...], axis=0)

    scatter(0, part0, got0)
    own = part0[w]
    mean_total = own[:, 2 * width:]
    for d in range(1, nw):
        mean_total = mean_total + got0[d, :, 2 * width:]
    energy_mean = mean_total[:, :1] / float(nw)
    delta = own[:, 2 * width:2 * width + 1] - energy_mean
    column_sum = own[:, width:2 * width]
    force = own[:, :width] + delta * own[:, width:2 * width]
    dev_sum = delta
    for d in range(1, nw):
        delta = got0[d, :, 2 * width:2 * width + 1] - energy_mean
        piece = got0[d, :, width:2 * width]
        column_sum = column_sum + piece
        force = force + got0[d, :, :width] + delta * piece
        dev_sum = dev_sum + delta
    column_mean = column_sum / walkers
    base[w, :, :width] = (force - column_mean * (dev_sum * float(LANE))) / walkers
    base[w, :, width:] = column_mean

    zero_row = jnp.zeros((1, LANE), jnp.float32)

    def fresh(count):
        return jnp.zeros((LANE, LANE), jnp.float32), zero_row, (zero_row,) * count

    def project(k, carry, vector, others):
        total, centre, dots = carry
        for b in range(blocks):
            at = slice(b * LANE, (b + 1) * LANE)
            row = vector[k, :, at]
            block = jac[:, pl.ds(pl.multiple_of(k * width + b * LANE, LANE), LANE)]
            total = total + block * row
            centre = centre + base[k, :, width + b * LANE:width + (b + 1) * LANE] * row
            dots = tuple(dot + other[k, :, at] * row for dot, other in zip(dots, others))
        return total, centre, dots

    def message(carry):
        total, centre, dots = carry
        row = jnp.sum(jnp.transpose(total), axis=0, keepdims=True)
        centre = jnp.sum(centre, axis=1, keepdims=True)
        dots = [jnp.sum(dot, axis=1, keepdims=True) for dot in dots]
        return jnp.concatenate([row - centre, lane_pack(lane, dots)], axis=1)

    def spread(number, weights, scalars):
        column = as_column(weights)
        small, large = sums_buf.at[number], full.at[number]
        small[0] = lane_pack(lane, scalars)

        def small_copy(d):
            return pltpu.make_async_remote_copy(
                src_ref=small.at[0], dst_ref=small.at[d], send_sem=small_send.at[number],
                recv_sem=small_recv.at[number], device_id=walk_peer(d), device_id_type=MESH)
        each(nw, lambda d: small_copy(d).start())

        def step(k, carry):
            for b in range(blocks):
                block = jac[:, pl.ds(pl.multiple_of(k * width + b * LANE, LANE), LANE)]
                large[k, 0, :, b * LANE:(b + 1) * LANE] = jnp.sum(block * column, axis=0, keepdims=True)
            each(nw, lambda d: pltpu.make_async_remote_copy(
                src_ref=large.at[k, 0], dst_ref=large.at[k, d], send_sem=full_send.at[number, k],
                recv_sem=full_recv.at[number, k], device_id=walk_peer(d), device_id_type=MESH).start())
            return carry
        lax.fori_loop(0, nw, step, 0)

    def walk_sums(number):
        whole = all_of(sums_buf.at[number], small_send.at[number], small_recv.at[number])
        whole.wait_recv()
        whole.wait_send()
        return jnp.sum(sums_buf[number], axis=0)

    def absorb(number, vector, advance, others):
        def step(k, carry):
            all_of(full.at[number, k], full_send.at[number, k], full_recv.at[number, k]).wait_recv()
            image = jnp.sum(full[number, k], axis=0) / walkers
            vector[k] = advance(k, image)
            return project(k, carry, vector, others)
        carry = lax.fori_loop(0, nw, step, fresh(len(others)))
        for k in range(nw):
            all_of(full.at[number, k], full_send.at[number, k], full_recv.at[number, k]).wait_send()
        return message(carry)

    seed_shift = shift_ref[0]

    def gather_copy(d, dst):
        return pltpu.make_async_remote_copy(
            src_ref=base.at[w], dst_ref=dst, send_sem=walk_send.at[d], recv_sem=walk_recv.at[1, d],
            device_id=walk_peer(d), device_id_type=MESH)
    each(nw, lambda d: gather_copy(d, base.at[w]).start())

    def first_step(d, carry):
        k = lax.rem(w + nw - d, nw)
        gather_copy(d, base.at[k]).wait_recv()
        return project(k, carry, base, (base,))
    carry = lax.fori_loop(1, nw, first_step, project(w, fresh(1), base, (base,)))
    each(nw, lambda d: gather_copy(d, base.at[w]).wait_send())

    reply = param_sum(0, message(carry))
    q0, m00 = reply[:, :LANE], lane_pick(reply[:, LANE:], lane, 0)
    spread(0, q0, [dot_row(q0, q0)])
    k00 = lane_pick(walk_sums(0), lane, 0) / walkers
    step0 = m00 / (k00 + seed_shift * m00)

    def advance0(k, image):
        r0 = base[k, :, :width]
        return r0 - step0 * (image + seed_shift * r0)

    reply = direct_sum(1, absorb(0, next1, advance0, (next1, base)))
    q1, sums = reply[:, :LANE], reply[:, LANE:]
    m11, m01 = lane_pick(sums, lane, 0), lane_pick(sums, lane, 1)
    turn = m11 / m00
    p1 = q1 + turn * q0
    spread(1, p1, [dot_row(q1, q1), dot_row(q0, q1), dot_row(p1, p1)])
    sums = walk_sums(1)
    k11, k01, pp1 = (lane_pick(sums, lane, i) / walkers for i in range(3))
    dd1 = m11 + 2.0 * turn * m01 + turn * turn * m00
    step1 = m11 / (pp1 + seed_shift * dd1)

    def advance1(k, image):
        r1 = next1[k]
        return r1 - step1 * (image + seed_shift * (r1 + turn * base[k, :, :width]))

    reply = direct_sum(2, absorb(1, next2, advance1, (next2, base, next1)))
    q2, sums = reply[:, :LANE], reply[:, LANE:]
    m22, m02, m12 = (lane_pick(sums, lane, i) for i in range(3))
    small = sums_buf.at[2]
    small[0] = lane_pack(lane, [dot_row(q2, q2), dot_row(q0, q2), dot_row(q1, q2)])
    each(nw, lambda d: pltpu.make_async_remote_copy(
        src_ref=small.at[0], dst_ref=small.at[d], send_sem=small_send.at[2],
        recv_sem=small_recv.at[2], device_id=walk_peer(d), device_id_type=MESH).start())
    sums = walk_sums(2)
    k22, k02, k12 = (lane_pick(sums, lane, i) / walkers for i in range(3))

    count = out_ref.shape[0]
    trial = lax.broadcasted_iota(jnp.int32, (count, LANE), 0)
    shift = jnp.zeros((count, LANE), jnp.float32)
    for number in range(count):
        shift = jnp.where(trial == number, shift_ref[number], shift)
    a00, a01, a02 = k00 + shift * m00, k01 + shift * m01, k02 + shift * m02
    a11, a12, a22 = k11 + shift * m11, k12 + shift * m12, k22 + shift * m22
    l10, l20 = a01 / a00, a02 / a00
    e1 = a11 - l10 * a01
    e21 = a12 - l20 * a01
    l21 = e21 / e1
    e2 = a22 - l20 * a02 - l21 * e21
    b1 = m01 - l10 * m00
    b2 = m02 - l20 * m00 - l21 * b1
    c2 = b2 / e2
    c1 = b1 / e1 - l21 * c2
    c0 = m00 / a00 - l10 * c1 - l20 * c2
    square = c0 * (c0 * m00 + 2.0 * (c1 * m01 + c2 * m02)) + c1 * (c1 * m11 + 2.0 * c2 * m12) + c2 * c2 * m22
    scale = lax.rsqrt(square / params + EPSILON)
    c0, c1, c2 = c0 * scale, c1 * scale, c2 * scale

    def write(k, b):
        at = slice(b * LANE, (b + 1) * LANE)
        out_ref[:, pl.ds(pl.multiple_of(k * width + b * LANE, LANE), LANE)] = (
            c0 * base[k, :, at] + c1 * next1[k, :, at] + c2 * next2[k, :, at])

    whole = cols // width

    def write_piece(k, carry):
        for b in range(blocks):
            write(k, b)
        return carry
    lax.fori_loop(0, whole, write_piece, 0)
    for b in range((cols - whole * width) // LANE):
        write(whole, b)


def solution(mesh):
    nw, npar = mesh.shape["walk"], mesh.shape["param"]
    ny = Y_SIZE
    nz = npar // ny

    def body(jacobian, energies, shifts):
        cols = jacobian.shape[1]
        blocks = -(-(cols // LANE) // nw)
        width = blocks * LANE
        count = shifts.shape[0]
        f32 = jnp.float32
        return pl.pallas_call(
            functools.partial(kernel, (nw, ny, nz, cols, blocks)),
            out_shape=jax.ShapeDtypeStruct((count, cols), f32),
            in_specs=[
                pl.BlockSpec(memory_space=pl.ANY),
                pl.BlockSpec(memory_space=pl.ANY),
                pl.BlockSpec(memory_space=pl.ANY),
            ],
            out_specs=pl.BlockSpec(memory_space=pltpu.VMEM),
            scratch_shapes=[
                pltpu.VMEM((LANE, nw * width), f32),
                pltpu.VMEM((1, LANE), f32),
                pltpu.SMEM((count,), f32),
                pltpu.VMEM((nw, 1, 2 * width + LANE), f32),
                pltpu.VMEM((nw, 1, 2 * width + LANE), f32),
                pltpu.VMEM((nw, 1, 2 * width), f32),
                pltpu.VMEM((nw, 1, width), f32),
                pltpu.VMEM((nw, 1, width), f32),
                pltpu.VMEM((2, nw, nw, 1, width), f32),
                pltpu.VMEM((3, nw, 1, LANE), f32),
                pltpu.VMEM((3, ny, 1, 2 * LANE), f32),
                pltpu.VMEM((3, nz, 1, 2 * LANE), f32),
                pltpu.VMEM((2, ny * nz, 1, 2 * LANE), f32),
                pltpu.SemaphoreType.DMA((3,)),
                pltpu.SemaphoreType.DMA((nw,)),
                pltpu.SemaphoreType.DMA((2, nw)),
                pltpu.SemaphoreType.DMA((2, nw)),
                pltpu.SemaphoreType.DMA((2, nw)),
                pltpu.SemaphoreType.DMA((3,)),
                pltpu.SemaphoreType.DMA((3,)),
                pltpu.SemaphoreType.DMA((3, 2)),
                pltpu.SemaphoreType.DMA((3, 2)),
            ],
            compiler_params=pltpu.CompilerParams(
                collective_id=0, has_side_effects=True, vmem_limit_bytes=67043328
            ),
        )(jacobian, energies.reshape(1, -1), shifts)

    return jax.shard_map(
        body,
        mesh=mesh,
        in_specs=(P("walk", "param"), P("walk"), P()),
        out_specs=P(None, "param"),
        check_vma=False,
    )
```

```python
import functools

import jax
import jax.numpy as jnp
from jax import lax
from jax.experimental import pallas as pl
from jax.experimental.pallas import tpu as pltpu
from jax.sharding import PartitionSpec as P

EPSILON = 1e-06
LANE = 128
Y_SIZE = 4
MESH = pl.DeviceIdType.MESH


def lane_pick(row, lane, number):
    return jnp.sum(jnp.where(lane == number, row, 0.0), axis=1, keepdims=True)


def lane_pack(lane, values):
    row = jnp.zeros(lane.shape, jnp.float32)
    for number, value in enumerate(values):
        row = jnp.where(lane == number, value, row)
    return row


def dot_row(left, right):
    return jnp.sum(left * right, axis=1, keepdims=True)


def as_column(row):
    return jnp.transpose(jnp.broadcast_to(row, (LANE, LANE)))


def kernel(
    dims,
    jac_hbm, energy_hbm, shift_hbm, out_ref,
    jac, energy_ref, shift_ref, part0, got0, base, next1, next2, image_buf, full, sums_buf,
    ybuf, zbuf, wide, load_sem, walk_send, walk_recv, full_send, full_recv, small_send, small_recv,
    param_send, param_recv, hello,
):
    nw, ny, nz, cols, blocks = dims
    width = blocks * LANE
    walkers = float(nw * LANE)
    params = float(ny * nz * cols)
    w = lax.axis_index("walk")
    p = lax.axis_index("param")
    y, z = lax.rem(p, ny), p // ny

    load_energy = pltpu.make_async_copy(energy_hbm, energy_ref, load_sem.at[nw])
    load_shift = pltpu.make_async_copy(shift_hbm, shift_ref, load_sem.at[nw + 1])
    filled = cols // width

    def load(k, size):
        to = pl.ds(pl.multiple_of(k * width, LANE), size)
        return pltpu.make_async_copy(jac_hbm.at[:, to], jac.at[:, to], load_sem.at[k])

    loads = [load(k, min(width, cols - k * width)) for k in range(nw) if k * width < cols]
    load_energy.start()
    load_shift.start()
    for copy in loads:
        copy.start()

    barrier = pltpu.get_barrier_semaphore()

    def walk_peer(d):
        return (lax.rem(w + d, nw), p)

    def y_peer(d):
        return (w, z * ny + lax.rem(y + d, ny))

    def z_peer(d):
        return (w, lax.rem(z + d, nz) * ny + y)

    def each(count, step):
        def go(d, carry):
            step(d)
            return carry
        lax.fori_loop(1, count, go, 0)

    for count, peer in ((nw, walk_peer), (ny, y_peer), (nz, z_peer)):
        each(count, lambda d, peer=peer: pl.semaphore_signal(
            barrier, inc=1, device_id=peer(d), device_id_type=MESH))

    if nw * width > cols:
        jac[:, cols:] = jnp.zeros((LANE, nw * width - cols), jnp.float32)

    lane = lax.broadcasted_iota(jnp.int32, (1, LANE), 1)
    load_energy.wait()
    load_shift.wait()
    energy = energy_ref[...]
    group_mean = jnp.sum(energy, axis=1, keepdims=True) / float(LANE)
    energy_col = as_column(energy - group_mean)
    mean_row = jnp.broadcast_to(group_mean, (1, LANE))

    def first_pass(k):
        for b in range(blocks):
            block = jac[:, pl.ds(pl.multiple_of(k * width + b * LANE, LANE), LANE)]
            part0[k, :, b * LANE:(b + 1) * LANE] = jnp.sum(block * energy_col, axis=0, keepdims=True)
            part0[k, :, width + b * LANE:width + (b + 1) * LANE] = jnp.sum(block, axis=0, keepdims=True)
        part0[k, :, 2 * width:] = mean_row

    def first_full(k, carry):
        load(k, width).wait()
        first_pass(k)
        return carry
    lax.fori_loop(0, filled, first_full, 0)
    for k in range(filled, nw):
        if k < len(loads):
            loads[k].wait()
        first_pass(k)

    pl.semaphore_wait(barrier, (nw - 1) + (ny - 1) + (nz - 1))

    def exchange(count, source, target, landed, send, recv, peer):
        def copy(d, dst):
            return pltpu.make_async_remote_copy(
                src_ref=source(d), dst_ref=dst, send_sem=send.at[d], recv_sem=recv.at[d],
                device_id=peer(d), device_id_type=MESH)
        each(count, lambda d: copy(d, target(d)).start())
        each(count, lambda d: copy(d, landed(d)).wait_recv())
        each(count, lambda d: copy(d, target(d)).wait_send())

    def scatter(number, pieces, buffer):
        exchange(nw, lambda d: pieces.at[lax.rem(w + d, nw)], lambda d: buffer.at[d], lambda d: buffer.at[d],
                 walk_send, walk_recv.at[number], walk_peer)

    def far_first(count):
        return sorted(range(1, count), key=lambda d: -min(d, count - d))

    def all_of(buffer, send, recv):
        rest = buffer.at[pl.ds(1, buffer.shape[0] - 1)]
        return pltpu.make_async_remote_copy(
            src_ref=rest, dst_ref=rest, send_sem=send, recv_sem=recv,
            device_id=walk_peer(1), device_id_type=MESH)

    def spray(buffer, send, recv, count, peer):
        for d in far_first(count):
            pltpu.make_async_remote_copy(
                src_ref=buffer.at[0], dst_ref=buffer.at[d], send_sem=send, recv_sem=recv,
                device_id=peer(d), device_id_type=MESH).start()
        return all_of(buffer, send, recv)

    def param_sum(number, carry):
        total, centre, dots = carry
        row = jnp.sum(jnp.transpose(total), axis=0, keepdims=True)
        mine, ys, zs = wide.at[number], ybuf.at[number], zbuf.at[number]
        send, recv = param_send.at[number, 0], param_recv.at[number, 0]
        mine[0] = row - jnp.sum(centre, axis=1, keepdims=True)

        def start(dz, dy):
            pltpu.make_async_remote_copy(
                src_ref=mine.at[0], dst_ref=mine.at[dz * ny + dy], send_sem=send, recv_sem=recv,
                device_id=(w, lax.rem(z + dz, nz) * ny + lax.rem(y + dy, ny)), device_id_type=MESH).start()

        def go(i, carry):
            dz = nz // 2 + ((i + 1) // 2) * (1 - 2 * lax.rem(i, 2))
            for dy in far_first(ny) + [0]:
                start(dz, dy)
            return carry
        lax.fori_loop(0, nz - 1, go, 0)
        for dy in far_first(ny):
            start(0, dy)
        ys[0] = lane_pack(lane, [jnp.sum(dot, axis=1, keepdims=True) for dot in dots])
        first = spray(ys, param_send.at[number, 1], param_recv.at[number, 1], ny, y_peer)
        first.wait_recv()
        zs[0] = jnp.sum(ys[...], axis=0)
        spray(zs, param_send.at[number, 2], param_recv.at[number, 2], nz, z_peer)
        first.wait_send()
        whole = all_of(mine, send, recv)
        whole.wait_recv()
        whole.wait_send()
        return jnp.sum(mine[...], axis=0)

    def param_dots(number):
        whole = all_of(zbuf.at[number], param_send.at[number, 2], param_recv.at[number, 2])
        whole.wait_recv()
        whole.wait_send()
        return jnp.sum(zbuf[number], axis=0)

    for d in far_first(ny):
        pl.semaphore_signal(hello, inc=1, device_id=y_peer(d), device_id_type=MESH)

    scatter(0, part0, got0)
    own = part0[w]
    mean_total = own[:, 2 * width:]
    for d in range(1, nw):
        mean_total = mean_total + got0[d, :, 2 * width:]
    energy_mean = mean_total[:, :1] / float(nw)
    delta = own[:, 2 * width:2 * width + 1] - energy_mean
    column_sum = own[:, width:2 * width]
    force = own[:, :width] + delta * own[:, width:2 * width]
    dev_sum = delta
    for d in range(1, nw):
        delta = got0[d, :, 2 * width:2 * width + 1] - energy_mean
        piece = got0[d, :, width:2 * width]
        column_sum = column_sum + piece
        force = force + got0[d, :, :width] + delta * piece
        dev_sum = dev_sum + delta
    column_mean = column_sum / walkers
    base[w, :, :width] = (force - column_mean * (dev_sum * float(LANE))) / walkers
    base[w, :, width:] = column_mean

    zero_row = jnp.zeros((1, LANE), jnp.float32)

    def fresh(count):
        return jnp.zeros((LANE, LANE), jnp.float32), zero_row, (zero_row,) * count

    def project(k, carry, vector, others):
        total, centre, dots = carry
        for b in range(blocks):
            at = slice(b * LANE, (b + 1) * LANE)
            row = vector[k, :, at]
            block = jac[:, pl.ds(pl.multiple_of(k * width + b * LANE, LANE), LANE)]
            total = total + block * row
            centre = centre + base[k, :, width + b * LANE:width + (b + 1) * LANE] * row
            dots = tuple(dot + other[k, :, at] * row for dot, other in zip(dots, others))
        return total, centre, dots

    def spread(number, weights, scalars):
        column = as_column(weights)
        small, large = sums_buf.at[number], full.at[number]
        small[0] = lane_pack(lane, scalars)

        def small_copy(d):
            return pltpu.make_async_remote_copy(
                src_ref=small.at[0], dst_ref=small.at[d], send_sem=small_send.at[number],
                recv_sem=small_recv.at[number], device_id=walk_peer(d), device_id_type=MESH)
        each(nw, lambda d: small_copy(d).start())

        def step(k, carry):
            for b in range(blocks):
                block = jac[:, pl.ds(pl.multiple_of(k * width + b * LANE, LANE), LANE)]
                large[k, 0, :, b * LANE:(b + 1) * LANE] = jnp.sum(block * column, axis=0, keepdims=True)
            each(nw, lambda d: pltpu.make_async_remote_copy(
                src_ref=large.at[k, 0], dst_ref=large.at[k, d], send_sem=full_send.at[number, k],
                recv_sem=full_recv.at[number, k], device_id=walk_peer(d), device_id_type=MESH).start())
            return carry
        lax.fori_loop(0, nw, step, 0)

    def walk_sums(number):
        whole = all_of(sums_buf.at[number], small_send.at[number], small_recv.at[number])
        whole.wait_recv()
        whole.wait_send()
        return jnp.sum(sums_buf[number], axis=0)

    def absorb(number, vector, advance, others):
        def step(k, carry):
            all_of(full.at[number, k], full_send.at[number, k], full_recv.at[number, k]).wait_recv()
            image = jnp.sum(full[number, k], axis=0) / walkers
            vector[k] = advance(k, image)
            return project(k, carry, vector, others)
        carry = lax.fori_loop(0, nw, step, fresh(len(others)))
        for k in range(nw):
            all_of(full.at[number, k], full_send.at[number, k], full_recv.at[number, k]).wait_send()
        return carry

    seed_shift = shift_ref[0]

    def gather_copy(d, dst):
        return pltpu.make_async_remote_copy(
            src_ref=base.at[w], dst_ref=dst, send_sem=walk_send.at[d], recv_sem=walk_recv.at[1, d],
            device_id=walk_peer(d), device_id_type=MESH)
    each(nw, lambda d: gather_copy(d, base.at[w]).start())

    def first_step(d, carry):
        k = lax.rem(w + nw - d, nw)
        gather_copy(d, base.at[k]).wait_recv()
        return project(k, carry, base, (base,))
    carry = lax.fori_loop(1, nw, first_step, project(w, fresh(1), base, (base,)))
    each(nw, lambda d: gather_copy(d, base.at[w]).wait_send())

    pl.semaphore_wait(hello, ny - 1)
    q0 = param_sum(0, carry)
    spread(0, q0, [dot_row(q0, q0)])
    m00 = lane_pick(param_dots(0), lane, 0)
    k00 = lane_pick(walk_sums(0), lane, 0) / walkers
    step0 = m00 / (k00 + seed_shift * m00)

    def advance0(k, image):
        r0 = base[k, :, :width]
        image_buf[k] = image
        return r0 - step0 * (image + seed_shift * r0)

    q1 = param_sum(1, absorb(0, next1, advance0, (next1, base)))
    spread(1, q1, [dot_row(q1, q1), dot_row(q0, q1)])
    sums = param_dots(1)
    m11, m01 = lane_pick(sums, lane, 0), lane_pick(sums, lane, 1)
    turn = m11 / m00
    sums = walk_sums(1)
    k11, k01 = (lane_pick(sums, lane, i) / walkers for i in range(2))
    pp1 = k11 + turn * (2.0 * k01 + turn * k00)
    dd1 = m11 + turn * (2.0 * m01 + turn * m00)
    step1 = m11 / (pp1 + seed_shift * dd1)

    def advance1(k, image):
        r1 = next1[k]
        direction = r1 + turn * base[k, :, :width]
        return r1 - step1 * (image + turn * image_buf[k] + seed_shift * direction)

    q2 = param_sum(2, absorb(1, next2, advance1, (next2, base, next1)))
    small = sums_buf.at[2]
    small[0] = lane_pack(lane, [dot_row(q2, q2), dot_row(q0, q2), dot_row(q1, q2)])
    each(nw, lambda d: pltpu.make_async_remote_copy(
        src_ref=small.at[0], dst_ref=small.at[d], send_sem=small_send.at[2],
        recv_sem=small_recv.at[2], device_id=walk_peer(d), device_id_type=MESH).start())
    sums = walk_sums(2)
    dots = param_dots(2)
    m22, m02, m12 = (lane_pick(dots, lane, i) for i in range(3))
    k22, k02, k12 = (lane_pick(sums, lane, i) / walkers for i in range(3))

    count = out_ref.shape[0]
    trial = lax.broadcasted_iota(jnp.int32, (count, LANE), 0)
    shift = jnp.zeros((count, LANE), jnp.float32)
    for number in range(count):
        shift = jnp.where(trial == number, shift_ref[number], shift)
    a00, a01, a02 = k00 + shift * m00, k01 + shift * m01, k02 + shift * m02
    a11, a12, a22 = k11 + shift * m11, k12 + shift * m12, k22 + shift * m22
    l10, l20 = a01 / a00, a02 / a00
    e1 = a11 - l10 * a01
    e21 = a12 - l20 * a01
    l21 = e21 / e1
    e2 = a22 - l20 * a02 - l21 * e21
    b1 = m01 - l10 * m00
    b2 = m02 - l20 * m00 - l21 * b1
    c2 = b2 / e2
    c1 = b1 / e1 - l21 * c2
    c0 = m00 / a00 - l10 * c1 - l20 * c2
    square = c0 * (c0 * m00 + 2.0 * (c1 * m01 + c2 * m02)) + c1 * (c1 * m11 + 2.0 * c2 * m12) + c2 * c2 * m22
    scale = lax.rsqrt(square / params + EPSILON)
    c0, c1, c2 = c0 * scale, c1 * scale, c2 * scale

    def write(k, b):
        at = slice(b * LANE, (b + 1) * LANE)
        out_ref[:, pl.ds(pl.multiple_of(k * width + b * LANE, LANE), LANE)] = (
            c0 * base[k, :, at] + c1 * next1[k, :, at] + c2 * next2[k, :, at])

    whole = cols // width

    def write_piece(k, carry):
        for b in range(blocks):
            write(k, b)
        return carry
    lax.fori_loop(0, whole, write_piece, 0)
    for b in range((cols - whole * width) // LANE):
        write(whole, b)


def solution(mesh):
    nw, npar = mesh.shape["walk"], mesh.shape["param"]
    ny = Y_SIZE
    nz = npar // ny

    def body(jacobian, energies, shifts):
        cols = jacobian.shape[1]
        blocks = -(-(cols // LANE) // nw)
        width = blocks * LANE
        count = shifts.shape[0]
        f32 = jnp.float32
        return pl.pallas_call(
            functools.partial(kernel, (nw, ny, nz, cols, blocks)),
            out_shape=jax.ShapeDtypeStruct((count, cols), f32),
            in_specs=[
                pl.BlockSpec(memory_space=pl.ANY),
                pl.BlockSpec(memory_space=pl.ANY),
                pl.BlockSpec(memory_space=pl.ANY),
            ],
            out_specs=pl.BlockSpec(memory_space=pltpu.VMEM),
            scratch_shapes=[
                pltpu.VMEM((LANE, nw * width), f32),
                pltpu.VMEM((1, LANE), f32),
                pltpu.SMEM((count,), f32),
                pltpu.VMEM((nw, 1, 2 * width + LANE), f32),
                pltpu.VMEM((nw, 1, 2 * width + LANE), f32),
                pltpu.VMEM((nw, 1, 2 * width), f32),
                pltpu.VMEM((nw, 1, width), f32),
                pltpu.VMEM((nw, 1, width), f32),
                pltpu.VMEM((nw, 1, width), f32),
                pltpu.VMEM((2, nw, nw, 1, width), f32),
                pltpu.VMEM((3, nw, 1, LANE), f32),
                pltpu.VMEM((3, ny, 1, LANE), f32),
                pltpu.VMEM((3, nz, 1, LANE), f32),
                pltpu.VMEM((3, ny * nz, 1, LANE), f32),
                pltpu.SemaphoreType.DMA((nw + 2,)),
                pltpu.SemaphoreType.DMA((nw,)),
                pltpu.SemaphoreType.DMA((2, nw)),
                pltpu.SemaphoreType.DMA((2, nw)),
                pltpu.SemaphoreType.DMA((2, nw)),
                pltpu.SemaphoreType.DMA((3,)),
                pltpu.SemaphoreType.DMA((3,)),
                pltpu.SemaphoreType.DMA((3, 3)),
                pltpu.SemaphoreType.DMA((3, 3)),
                pltpu.SemaphoreType.REGULAR,
            ],
            compiler_params=pltpu.CompilerParams(
                collective_id=0, has_side_effects=True, vmem_limit_bytes=67043328
            ),
        )(jacobian, energies.reshape(1, -1), shifts)

    return jax.shard_map(
        body,
        mesh=mesh,
        in_specs=(P("walk", "param"), P("walk"), P()),
        out_specs=P(None, "param"),
        check_vma=False,
    )
```

```python
import functools

import jax
import jax.numpy as jnp
from jax import lax
from jax.experimental import pallas as pl
from jax.experimental.pallas import tpu as pltpu
from jax.sharding import PartitionSpec as P

EPSILON = 1e-06
LANE = 128
Y_SIZE = 4
MESH = pl.DeviceIdType.MESH


def lane_pick(row, lane, number):
    return jnp.sum(jnp.where(lane == number, row, 0.0), axis=1, keepdims=True)


def lane_pack(lane, values):
    row = jnp.zeros(lane.shape, jnp.float32)
    for number, value in enumerate(values):
        row = jnp.where(lane == number, value, row)
    return row


def dot_row(left, right):
    return jnp.sum(left * right, axis=1, keepdims=True)


def as_column(row):
    return jnp.transpose(jnp.broadcast_to(row, (LANE, LANE)))


def kernel(
    dims,
    jac_hbm, energy_hbm, shift_hbm, out_ref,
    jac, energy_ref, shift_ref, part0, got0, base, next1, next2, image_buf, full, sums_buf,
    ybuf, zbuf, wide, load_sem, walk_send, walk_recv, full_send, full_recv, small_send, small_recv,
    param_send, param_recv, hello,
):
    nw, ny, nz, cols, blocks = dims
    width = blocks * LANE
    walkers = float(nw * LANE)
    params = float(ny * nz * cols)
    w = lax.axis_index("walk")
    p = lax.axis_index("param")
    y, z = lax.rem(p, ny), p // ny

    load_energy = pltpu.make_async_copy(energy_hbm, energy_ref, load_sem.at[nw])
    load_shift = pltpu.make_async_copy(shift_hbm, shift_ref, load_sem.at[nw + 1])
    filled = cols // width

    def load(k, size):
        to = pl.ds(pl.multiple_of(k * width, LANE), size)
        return pltpu.make_async_copy(jac_hbm.at[:, to], jac.at[:, to], load_sem.at[k])

    loads = [load(k, min(width, cols - k * width)) for k in range(nw) if k * width < cols]
    load_energy.start()
    load_shift.start()
    for copy in loads:
        copy.start()

    barrier = pltpu.get_barrier_semaphore()

    def walk_peer(d):
        return (lax.rem(w + d, nw), p)

    def y_peer(d):
        return (w, z * ny + lax.rem(y + d, ny))

    def z_peer(d):
        return (w, lax.rem(z + d, nz) * ny + y)

    def each(count, step):
        def go(d, carry):
            step(d)
            return carry
        lax.fori_loop(1, count, go, 0)

    for count, peer in ((nw, walk_peer), (ny, y_peer), (nz, z_peer)):
        each(count, lambda d, peer=peer: pl.semaphore_signal(
            barrier, inc=1, device_id=peer(d), device_id_type=MESH))

    if nw * width > cols:
        jac[:, cols:] = jnp.zeros((LANE, nw * width - cols), jnp.float32)

    lane = lax.broadcasted_iota(jnp.int32, (1, LANE), 1)
    load_energy.wait()
    load_shift.wait()
    energy = energy_ref[...]
    group_mean = jnp.sum(energy, axis=1, keepdims=True) / float(LANE)
    energy_col = as_column(energy - group_mean)
    mean_row = jnp.broadcast_to(group_mean, (1, LANE))

    def first_pass(k):
        for b in range(blocks):
            block = jac[:, pl.ds(pl.multiple_of(k * width + b * LANE, LANE), LANE)]
            part0[k, :, b * LANE:(b + 1) * LANE] = jnp.sum(block * energy_col, axis=0, keepdims=True)
            part0[k, :, width + b * LANE:width + (b + 1) * LANE] = jnp.sum(block, axis=0, keepdims=True)
        part0[k, :, 2 * width:] = mean_row

    def first_full(k, carry):
        load(k, width).wait()
        first_pass(k)
        return carry
    lax.fori_loop(0, filled, first_full, 0)
    for k in range(filled, nw):
        if k < len(loads):
            loads[k].wait()
        first_pass(k)

    pl.semaphore_wait(barrier, (nw - 1) + (ny - 1) + (nz - 1))

    def far_first(count):
        return sorted(range(1, count), key=lambda d: -min(d, count - d))

    def each_far(count, step):
        for d in far_first(count):
            step(d)

    def exchange(count, source, target, landed, send, recv, peer):
        def copy(d, dst):
            return pltpu.make_async_remote_copy(
                src_ref=source(d), dst_ref=dst, send_sem=send.at[d], recv_sem=recv.at[d],
                device_id=peer(d), device_id_type=MESH)
        each_far(count, lambda d: copy(d, target(d)).start())
        each(count, lambda d: copy(d, landed(d)).wait_recv())
        each(count, lambda d: copy(d, target(d)).wait_send())

    def scatter(number, pieces, buffer):
        exchange(nw, lambda d: pieces.at[lax.rem(w + d, nw)], lambda d: buffer.at[d], lambda d: buffer.at[d],
                 walk_send, walk_recv.at[number], walk_peer)

    def all_of(buffer, send, recv):
        rest = buffer.at[pl.ds(1, buffer.shape[0] - 1)]
        return pltpu.make_async_remote_copy(
            src_ref=rest, dst_ref=rest, send_sem=send, recv_sem=recv,
            device_id=walk_peer(1), device_id_type=MESH)

    def spray(buffer, send, recv, count, peer):
        for d in far_first(count):
            pltpu.make_async_remote_copy(
                src_ref=buffer.at[0], dst_ref=buffer.at[d], send_sem=send, recv_sem=recv,
                device_id=peer(d), device_id_type=MESH).start()
        return all_of(buffer, send, recv)

    def param_sum(number, carry):
        total, centre, dots = carry
        row = jnp.sum(jnp.transpose(total), axis=0, keepdims=True)
        mine, ys, zs = wide.at[number], ybuf.at[number], zbuf.at[number]
        send, recv = param_send.at[number, 0], param_recv.at[number, 0]
        mine[0] = row - jnp.sum(centre, axis=1, keepdims=True)

        def start(dz, dy):
            pltpu.make_async_remote_copy(
                src_ref=mine.at[0], dst_ref=mine.at[dz * ny + dy], send_sem=send, recv_sem=recv,
                device_id=(w, lax.rem(z + dz, nz) * ny + lax.rem(y + dy, ny)), device_id_type=MESH).start()

        def go(i, carry):
            dz = nz // 2 + ((i + 1) // 2) * (1 - 2 * lax.rem(i, 2))
            for dy in far_first(ny) + [0]:
                start(dz, dy)
            return carry
        lax.fori_loop(0, nz - 1, go, 0)
        for dy in far_first(ny):
            start(0, dy)
        ys[0] = lane_pack(lane, [jnp.sum(dot, axis=1, keepdims=True) for dot in dots])
        first = spray(ys, param_send.at[number, 1], param_recv.at[number, 1], ny, y_peer)
        first.wait_recv()
        zs[0] = jnp.sum(ys[...], axis=0)
        spray(zs, param_send.at[number, 2], param_recv.at[number, 2], nz, z_peer)
        first.wait_send()
        whole = all_of(mine, send, recv)
        whole.wait_recv()
        whole.wait_send()
        return jnp.sum(mine[...], axis=0)

    def param_dots(number):
        whole = all_of(zbuf.at[number], param_send.at[number, 2], param_recv.at[number, 2])
        whole.wait_recv()
        whole.wait_send()
        return jnp.sum(zbuf[number], axis=0)

    for d in far_first(ny):
        pl.semaphore_signal(hello, inc=1, device_id=y_peer(d), device_id_type=MESH)

    scatter(0, part0, got0)
    own = part0[w]
    mean_total = own[:, 2 * width:]
    for d in range(1, nw):
        mean_total = mean_total + got0[d, :, 2 * width:]
    energy_mean = mean_total[:, :1] / float(nw)
    delta = own[:, 2 * width:2 * width + 1] - energy_mean
    column_sum = own[:, width:2 * width]
    force = own[:, :width] + delta * own[:, width:2 * width]
    dev_sum = delta
    for d in range(1, nw):
        delta = got0[d, :, 2 * width:2 * width + 1] - energy_mean
        piece = got0[d, :, width:2 * width]
        column_sum = column_sum + piece
        force = force + got0[d, :, :width] + delta * piece
        dev_sum = dev_sum + delta
    column_mean = column_sum / walkers
    base[w, :, :width] = (force - column_mean * (dev_sum * float(LANE))) / walkers
    base[w, :, width:] = column_mean

    zero_row = jnp.zeros((1, LANE), jnp.float32)

    def fresh(count):
        return jnp.zeros((LANE, LANE), jnp.float32), zero_row, (zero_row,) * count

    def project(k, carry, vector, others):
        total, centre, dots = carry
        for b in range(blocks):
            at = slice(b * LANE, (b + 1) * LANE)
            row = vector[k, :, at]
            block = jac[:, pl.ds(pl.multiple_of(k * width + b * LANE, LANE), LANE)]
            total = total + block * row
            centre = centre + base[k, :, width + b * LANE:width + (b + 1) * LANE] * row
            dots = tuple(dot + other[k, :, at] * row for dot, other in zip(dots, others))
        return total, centre, dots

    def spread(number, weights, scalars):
        column = as_column(weights)
        small, large = sums_buf.at[number], full.at[number]
        small[0] = lane_pack(lane, scalars)

        def small_copy(d):
            return pltpu.make_async_remote_copy(
                src_ref=small.at[0], dst_ref=small.at[d], send_sem=small_send.at[number],
                recv_sem=small_recv.at[number], device_id=walk_peer(d), device_id_type=MESH)
        each_far(nw, lambda d: small_copy(d).start())

        def step(k, carry):
            for b in range(blocks):
                block = jac[:, pl.ds(pl.multiple_of(k * width + b * LANE, LANE), LANE)]
                large[k, 0, :, b * LANE:(b + 1) * LANE] = jnp.sum(block * column, axis=0, keepdims=True)
            each_far(nw, lambda d: pltpu.make_async_remote_copy(
                src_ref=large.at[k, 0], dst_ref=large.at[k, d], send_sem=full_send.at[number, k],
                recv_sem=full_recv.at[number, k], device_id=walk_peer(d), device_id_type=MESH).start())
            return carry
        lax.fori_loop(0, nw, step, 0)

    def walk_sums(number):
        whole = all_of(sums_buf.at[number], small_send.at[number], small_recv.at[number])
        whole.wait_recv()
        whole.wait_send()
        return jnp.sum(sums_buf[number], axis=0)

    def absorb(number, vector, advance, others):
        def step(k, carry):
            all_of(full.at[number, k], full_send.at[number, k], full_recv.at[number, k]).wait_recv()
            image = jnp.sum(full[number, k], axis=0) / walkers
            vector[k] = advance(k, image)
            return project(k, carry, vector, others)
        carry = lax.fori_loop(0, nw, step, fresh(len(others)))
        for k in range(nw):
            all_of(full.at[number, k], full_send.at[number, k], full_recv.at[number, k]).wait_send()
        return carry

    seed_shift = shift_ref[0]

    def gather_copy(d, dst):
        return pltpu.make_async_remote_copy(
            src_ref=base.at[w], dst_ref=dst, send_sem=walk_send.at[d], recv_sem=walk_recv.at[1, d],
            device_id=walk_peer(d), device_id_type=MESH)
    each_far(nw, lambda d: gather_copy(d, base.at[w]).start())

    def first_step(d, carry):
        k = lax.rem(w + nw - d, nw)
        gather_copy(d, base.at[k]).wait_recv()
        return project(k, carry, base, (base,))
    carry = lax.fori_loop(1, nw, first_step, project(w, fresh(1), base, (base,)))
    each(nw, lambda d: gather_copy(d, base.at[w]).wait_send())

    pl.semaphore_wait(hello, ny - 1)
    q0 = param_sum(0, carry)
    spread(0, q0, [dot_row(q0, q0)])
    m00 = lane_pick(param_dots(0), lane, 0)
    k00 = lane_pick(walk_sums(0), lane, 0) / walkers
    step0 = m00 / (k00 + seed_shift * m00)

    def advance0(k, image):
        r0 = base[k, :, :width]
        image_buf[k] = image
        return r0 - step0 * (image + seed_shift * r0)

    q1 = param_sum(1, absorb(0, next1, advance0, (next1, base)))
    spread(1, q1, [dot_row(q1, q1), dot_row(q0, q1)])
    sums = param_dots(1)
    m11, m01 = lane_pick(sums, lane, 0), lane_pick(sums, lane, 1)
    turn = m11 / m00
    sums = walk_sums(1)
    k11, k01 = (lane_pick(sums, lane, i) / walkers for i in range(2))
    pp1 = k11 + turn * (2.0 * k01 + turn * k00)
    dd1 = m11 + turn * (2.0 * m01 + turn * m00)
    step1 = m11 / (pp1 + seed_shift * dd1)

    def advance1(k, image):
        r1 = next1[k]
        direction = r1 + turn * base[k, :, :width]
        return r1 - step1 * (image + turn * image_buf[k] + seed_shift * direction)

    q2 = param_sum(2, absorb(1, next2, advance1, (next2, base, next1)))
    small = sums_buf.at[2]
    small[0] = lane_pack(lane, [dot_row(q2, q2), dot_row(q0, q2), dot_row(q1, q2)])
    each_far(nw, lambda d: pltpu.make_async_remote_copy(
        src_ref=small.at[0], dst_ref=small.at[d], send_sem=small_send.at[2],
        recv_sem=small_recv.at[2], device_id=walk_peer(d), device_id_type=MESH).start())
    sums = walk_sums(2)
    dots = param_dots(2)
    m22, m02, m12 = (lane_pick(dots, lane, i) for i in range(3))
    k22, k02, k12 = (lane_pick(sums, lane, i) / walkers for i in range(3))

    count = out_ref.shape[0]
    trial = lax.broadcasted_iota(jnp.int32, (count, LANE), 0)
    shift = jnp.zeros((count, LANE), jnp.float32)
    for number in range(count):
        shift = jnp.where(trial == number, shift_ref[number], shift)
    a00, a01, a02 = k00 + shift * m00, k01 + shift * m01, k02 + shift * m02
    a11, a12, a22 = k11 + shift * m11, k12 + shift * m12, k22 + shift * m22
    l10, l20 = a01 / a00, a02 / a00
    e1 = a11 - l10 * a01
    e21 = a12 - l20 * a01
    l21 = e21 / e1
    e2 = a22 - l20 * a02 - l21 * e21
    b1 = m01 - l10 * m00
    b2 = m02 - l20 * m00 - l21 * b1
    c2 = b2 / e2
    c1 = b1 / e1 - l21 * c2
    c0 = m00 / a00 - l10 * c1 - l20 * c2
    square = c0 * (c0 * m00 + 2.0 * (c1 * m01 + c2 * m02)) + c1 * (c1 * m11 + 2.0 * c2 * m12) + c2 * c2 * m22
    scale = lax.rsqrt(square / params + EPSILON)
    c0, c1, c2 = c0 * scale, c1 * scale, c2 * scale

    def write(k, b):
        at = slice(b * LANE, (b + 1) * LANE)
        out_ref[:, pl.ds(pl.multiple_of(k * width + b * LANE, LANE), LANE)] = (
            c0 * base[k, :, at] + c1 * next1[k, :, at] + c2 * next2[k, :, at])

    whole = cols // width

    def write_piece(k, carry):
        for b in range(blocks):
            write(k, b)
        return carry
    lax.fori_loop(0, whole, write_piece, 0)
    for b in range((cols - whole * width) // LANE):
        write(whole, b)


def solution(mesh):
    nw, npar = mesh.shape["walk"], mesh.shape["param"]
    ny = Y_SIZE
    nz = npar // ny

    def body(jacobian, energies, shifts):
        cols = jacobian.shape[1]
        blocks = -(-(cols // LANE) // nw)
        width = blocks * LANE
        count = shifts.shape[0]
        f32 = jnp.float32
        return pl.pallas_call(
            functools.partial(kernel, (nw, ny, nz, cols, blocks)),
            out_shape=jax.ShapeDtypeStruct((count, cols), f32),
            in_specs=[
                pl.BlockSpec(memory_space=pl.ANY),
                pl.BlockSpec(memory_space=pl.ANY),
                pl.BlockSpec(memory_space=pl.ANY),
            ],
            out_specs=pl.BlockSpec(memory_space=pltpu.VMEM),
            scratch_shapes=[
                pltpu.VMEM((LANE, nw * width), f32),
                pltpu.VMEM((1, LANE), f32),
                pltpu.SMEM((count,), f32),
                pltpu.VMEM((nw, 1, 2 * width + LANE), f32),
                pltpu.VMEM((nw, 1, 2 * width + LANE), f32),
                pltpu.VMEM((nw, 1, 2 * width), f32),
                pltpu.VMEM((nw, 1, width), f32),
                pltpu.VMEM((nw, 1, width), f32),
                pltpu.VMEM((nw, 1, width), f32),
                pltpu.VMEM((2, nw, nw, 1, width), f32),
                pltpu.VMEM((3, nw, 1, LANE), f32),
                pltpu.VMEM((3, ny, 1, LANE), f32),
                pltpu.VMEM((3, nz, 1, LANE), f32),
                pltpu.VMEM((3, ny * nz, 1, LANE), f32),
                pltpu.SemaphoreType.DMA((nw + 2,)),
                pltpu.SemaphoreType.DMA((nw,)),
                pltpu.SemaphoreType.DMA((2, nw)),
                pltpu.SemaphoreType.DMA((2, nw)),
                pltpu.SemaphoreType.DMA((2, nw)),
                pltpu.SemaphoreType.DMA((3,)),
                pltpu.SemaphoreType.DMA((3,)),
                pltpu.SemaphoreType.DMA((3, 3)),
                pltpu.SemaphoreType.DMA((3, 3)),
                pltpu.SemaphoreType.REGULAR,
            ],
            compiler_params=pltpu.CompilerParams(
                collective_id=0, has_side_effects=True, vmem_limit_bytes=67043328
            ),
        )(jacobian, energies.reshape(1, -1), shifts)

    return jax.shard_map(
        body,
        mesh=mesh,
        in_specs=(P("walk", "param"), P("walk"), P()),
        out_specs=P(None, "param"),
        check_vma=False,
    )
```

```python
import functools

import jax
import jax.numpy as jnp
from jax import lax
from jax.experimental import pallas as pl
from jax.experimental.pallas import tpu as pltpu
from jax.sharding import PartitionSpec as P

EPSILON = 1e-06
LANE = 128
Y_SIZE = 4
MESH = pl.DeviceIdType.MESH


def lane_pick(row, lane, number):
    return jnp.sum(jnp.where(lane == number, row, 0.0), axis=1, keepdims=True)


def lane_pack(lane, values):
    row = jnp.zeros(lane.shape, jnp.float32)
    for number, value in enumerate(values):
        row = jnp.where(lane == number, value, row)
    return row


def dot_row(left, right):
    return jnp.sum(left * right, axis=1, keepdims=True)


def as_column(row):
    return jnp.transpose(jnp.broadcast_to(row, (LANE, LANE)))


def kernel(
    dims,
    jac_hbm, energy_hbm, shift_hbm, out_ref,
    jac, energy_ref, shift_ref, part0, got0, base, next1, next2, image_buf, full, sums_buf,
    ybuf, zbuf, wide, load_sem, walk_send, walk_recv, full_send, full_recv, small_send, small_recv,
    param_send, param_recv, hello,
):
    nw, ny, nz, cols, blocks = dims
    width = blocks * LANE
    walkers = float(nw * LANE)
    params = float(ny * nz * cols)
    w = lax.axis_index("walk")
    p = lax.axis_index("param")
    y, z = lax.rem(p, ny), p // ny

    load_energy = pltpu.make_async_copy(energy_hbm, energy_ref, load_sem.at[nw])
    load_shift = pltpu.make_async_copy(shift_hbm, shift_ref, load_sem.at[nw + 1])
    filled = cols // width

    def load(k, size):
        to = pl.ds(pl.multiple_of(k * width, LANE), size)
        return pltpu.make_async_copy(jac_hbm.at[:, to], jac.at[:, to], load_sem.at[k])

    loads = [load(k, min(width, cols - k * width)) for k in range(nw) if k * width < cols]
    load_energy.start()
    load_shift.start()
    for copy in loads:
        copy.start()

    barrier = pltpu.get_barrier_semaphore()

    def walk_peer(d):
        return (lax.rem(w + d, nw), p)

    def y_peer(d):
        return (w, z * ny + lax.rem(y + d, ny))

    def z_peer(d):
        return (w, lax.rem(z + d, nz) * ny + y)

    def each(count, step):
        def go(d, carry):
            step(d)
            return carry
        lax.fori_loop(1, count, go, 0)

    for count, peer in ((nw, walk_peer), (ny, y_peer), (nz, z_peer)):
        each(count, lambda d, peer=peer: pl.semaphore_signal(
            barrier, inc=1, device_id=peer(d), device_id_type=MESH))

    if nw * width > cols:
        jac[:, cols:] = jnp.zeros((LANE, nw * width - cols), jnp.float32)

    lane = lax.broadcasted_iota(jnp.int32, (1, LANE), 1)
    load_energy.wait()
    load_shift.wait()
    energy = energy_ref[...]
    group_mean = jnp.sum(energy, axis=1, keepdims=True) / float(LANE)
    energy_col = as_column(energy - group_mean)
    mean_row = jnp.broadcast_to(group_mean, (1, LANE))

    def first_pass(k):
        for b in range(blocks):
            block = jac[:, pl.ds(pl.multiple_of(k * width + b * LANE, LANE), LANE)]
            part0[k, :, b * LANE:(b + 1) * LANE] = jnp.sum(block * energy_col, axis=0, keepdims=True)
            part0[k, :, width + b * LANE:width + (b + 1) * LANE] = jnp.sum(block, axis=0, keepdims=True)
        part0[k, :, 2 * width:] = mean_row

    def first_full(k, carry):
        load(k, width).wait()
        first_pass(k)
        return carry
    lax.fori_loop(0, filled, first_full, 0)
    for k in range(filled, nw):
        if k < len(loads):
            loads[k].wait()
        first_pass(k)

    pl.semaphore_wait(barrier, (nw - 1) + (ny - 1) + (nz - 1))

    def far_first(count):
        return sorted(range(1, count), key=lambda d: -min(d, count - d))

    def each_far(count, step):
        for d in far_first(count):
            step(d)

    def exchange(count, source, target, landed, send, recv, peer):
        def copy(d, dst):
            return pltpu.make_async_remote_copy(
                src_ref=source(d), dst_ref=dst, send_sem=send.at[d], recv_sem=recv.at[d],
                device_id=peer(d), device_id_type=MESH)
        each_far(count, lambda d: copy(d, target(d)).start())
        each(count, lambda d: copy(d, landed(d)).wait_recv())
        each(count, lambda d: copy(d, target(d)).wait_send())

    def scatter(number, pieces, buffer):
        exchange(nw, lambda d: pieces.at[lax.rem(w + d, nw)], lambda d: buffer.at[d], lambda d: buffer.at[d],
                 walk_send, walk_recv.at[number], walk_peer)

    def all_of(buffer, send, recv):
        rest = buffer.at[pl.ds(1, buffer.shape[0] - 1)]
        return pltpu.make_async_remote_copy(
            src_ref=rest, dst_ref=rest, send_sem=send, recv_sem=recv,
            device_id=walk_peer(1), device_id_type=MESH)

    def spray(buffer, send, recv, count, peer):
        for d in far_first(count):
            pltpu.make_async_remote_copy(
                src_ref=buffer.at[0], dst_ref=buffer.at[d], send_sem=send, recv_sem=recv,
                device_id=peer(d), device_id_type=MESH).start()
        return all_of(buffer, send, recv)

    def param_sum(number, carry):
        total, centre, dots = carry
        row = jnp.sum(jnp.transpose(total), axis=0, keepdims=True)
        mine, ys, zs = wide.at[number], ybuf.at[number], zbuf.at[number]
        send, recv = param_send.at[number, 0], param_recv.at[number, 0]
        mine[0] = row - jnp.sum(centre, axis=1, keepdims=True)

        def start(dz, dy):
            pltpu.make_async_remote_copy(
                src_ref=mine.at[0], dst_ref=mine.at[dz * ny + dy], send_sem=send, recv_sem=recv,
                device_id=(w, lax.rem(z + dz, nz) * ny + lax.rem(y + dy, ny)), device_id_type=MESH).start()

        def go(i, carry):
            dz = nz // 2 + ((i + 1) // 2) * (1 - 2 * lax.rem(i, 2))
            for dy in far_first(ny) + [0]:
                start(dz, dy)
            return carry
        for dz in far_first(nz):
            for dy in far_first(ny) + [0]:
                start(dz, dy)
        for dy in far_first(ny):
            start(0, dy)
        ys[0] = lane_pack(lane, [jnp.sum(dot, axis=1, keepdims=True) for dot in dots])
        first = spray(ys, param_send.at[number, 1], param_recv.at[number, 1], ny, y_peer)
        first.wait_recv()
        zs[0] = jnp.sum(ys[...], axis=0)
        spray(zs, param_send.at[number, 2], param_recv.at[number, 2], nz, z_peer)
        first.wait_send()
        whole = all_of(mine, send, recv)
        whole.wait_recv()
        whole.wait_send()
        return jnp.sum(mine[...], axis=0)

    def param_dots(number):
        whole = all_of(zbuf.at[number], param_send.at[number, 2], param_recv.at[number, 2])
        whole.wait_recv()
        whole.wait_send()
        return jnp.sum(zbuf[number], axis=0)

    for d in far_first(ny):
        pl.semaphore_signal(hello, inc=1, device_id=y_peer(d), device_id_type=MESH)

    scatter(0, part0, got0)
    own = part0[w]
    mean_total = own[:, 2 * width:]
    for d in range(1, nw):
        mean_total = mean_total + got0[d, :, 2 * width:]
    energy_mean = mean_total[:, :1] / float(nw)
    delta = own[:, 2 * width:2 * width + 1] - energy_mean
    column_sum = own[:, width:2 * width]
    force = own[:, :width] + delta * own[:, width:2 * width]
    dev_sum = delta
    for d in range(1, nw):
        delta = got0[d, :, 2 * width:2 * width + 1] - energy_mean
        piece = got0[d, :, width:2 * width]
        column_sum = column_sum + piece
        force = force + got0[d, :, :width] + delta * piece
        dev_sum = dev_sum + delta
    column_mean = column_sum / walkers
    base[w, :, :width] = (force - column_mean * (dev_sum * float(LANE))) / walkers
    base[w, :, width:] = column_mean

    zero_row = jnp.zeros((1, LANE), jnp.float32)

    def fresh(count):
        return jnp.zeros((LANE, LANE), jnp.float32), zero_row, (zero_row,) * count

    def project(k, carry, vector, others):
        total, centre, dots = carry
        for b in range(blocks):
            at = slice(b * LANE, (b + 1) * LANE)
            row = vector[k, :, at]
            block = jac[:, pl.ds(pl.multiple_of(k * width + b * LANE, LANE), LANE)]
            total = total + block * row
            centre = centre + base[k, :, width + b * LANE:width + (b + 1) * LANE] * row
            dots = tuple(dot + other[k, :, at] * row for dot, other in zip(dots, others))
        return total, centre, dots

    def spread(number, weights, scalars):
        column = as_column(weights)
        small, large = sums_buf.at[number], full.at[number]
        small[0] = lane_pack(lane, scalars)

        def small_copy(d):
            return pltpu.make_async_remote_copy(
                src_ref=small.at[0], dst_ref=small.at[d], send_sem=small_send.at[number],
                recv_sem=small_recv.at[number], device_id=walk_peer(d), device_id_type=MESH)
        each_far(nw, lambda d: small_copy(d).start())

        def step(k, carry):
            for b in range(blocks):
                block = jac[:, pl.ds(pl.multiple_of(k * width + b * LANE, LANE), LANE)]
                large[k, 0, :, b * LANE:(b + 1) * LANE] = jnp.sum(block * column, axis=0, keepdims=True)
            each_far(nw, lambda d: pltpu.make_async_remote_copy(
                src_ref=large.at[k, 0], dst_ref=large.at[k, d], send_sem=full_send.at[number, k],
                recv_sem=full_recv.at[number, k], device_id=walk_peer(d), device_id_type=MESH).start())
            return carry
        lax.fori_loop(0, nw, step, 0)

    def walk_sums(number):
        whole = all_of(sums_buf.at[number], small_send.at[number], small_recv.at[number])
        whole.wait_recv()
        whole.wait_send()
        return jnp.sum(sums_buf[number], axis=0)

    def absorb(number, vector, advance, others):
        def step(k, carry):
            all_of(full.at[number, k], full_send.at[number, k], full_recv.at[number, k]).wait_recv()
            image = jnp.sum(full[number, k], axis=0) / walkers
            vector[k] = advance(k, image)
            return project(k, carry, vector, others)
        carry = lax.fori_loop(0, nw, step, fresh(len(others)))
        for k in range(nw):
            all_of(full.at[number, k], full_send.at[number, k], full_recv.at[number, k]).wait_send()
        return carry

    seed_shift = shift_ref[0]

    def gather_copy(d, dst):
        return pltpu.make_async_remote_copy(
            src_ref=base.at[w], dst_ref=dst, send_sem=walk_send.at[d], recv_sem=walk_recv.at[1, d],
            device_id=walk_peer(d), device_id_type=MESH)
    each_far(nw, lambda d: gather_copy(d, base.at[w]).start())

    def first_step(d, carry):
        k = lax.rem(w + nw - d, nw)
        gather_copy(d, base.at[k]).wait_recv()
        return project(k, carry, base, (base,))
    carry = lax.fori_loop(1, nw, first_step, project(w, fresh(1), base, (base,)))
    each(nw, lambda d: gather_copy(d, base.at[w]).wait_send())

    pl.semaphore_wait(hello, ny - 1)
    q0 = param_sum(0, carry)
    spread(0, q0, [dot_row(q0, q0)])
    m00 = lane_pick(param_dots(0), lane, 0)
    k00 = lane_pick(walk_sums(0), lane, 0) / walkers
    step0 = m00 / (k00 + seed_shift * m00)

    def advance0(k, image):
        r0 = base[k, :, :width]
        image_buf[k] = image
        return r0 - step0 * (image + seed_shift * r0)

    q1 = param_sum(1, absorb(0, next1, advance0, (next1, base)))
    spread(1, q1, [dot_row(q1, q1), dot_row(q0, q1)])
    sums = param_dots(1)
    m11, m01 = lane_pick(sums, lane, 0), lane_pick(sums, lane, 1)
    turn = m11 / m00
    sums = walk_sums(1)
    k11, k01 = (lane_pick(sums, lane, i) / walkers for i in range(2))
    pp1 = k11 + turn * (2.0 * k01 + turn * k00)
    dd1 = m11 + turn * (2.0 * m01 + turn * m00)
    step1 = m11 / (pp1 + seed_shift * dd1)

    def advance1(k, image):
        r1 = next1[k]
        direction = r1 + turn * base[k, :, :width]
        return r1 - step1 * (image + turn * image_buf[k] + seed_shift * direction)

    q2 = param_sum(2, absorb(1, next2, advance1, (next2, base, next1)))
    small = sums_buf.at[2]
    small[0] = lane_pack(lane, [dot_row(q2, q2), dot_row(q0, q2), dot_row(q1, q2)])
    each_far(nw, lambda d: pltpu.make_async_remote_copy(
        src_ref=small.at[0], dst_ref=small.at[d], send_sem=small_send.at[2],
        recv_sem=small_recv.at[2], device_id=walk_peer(d), device_id_type=MESH).start())
    sums = walk_sums(2)
    dots = param_dots(2)
    m22, m02, m12 = (lane_pick(dots, lane, i) for i in range(3))
    k22, k02, k12 = (lane_pick(sums, lane, i) / walkers for i in range(3))

    count = out_ref.shape[0]
    trial = lax.broadcasted_iota(jnp.int32, (count, LANE), 0)
    shift = jnp.zeros((count, LANE), jnp.float32)
    for number in range(count):
        shift = jnp.where(trial == number, shift_ref[number], shift)
    a00, a01, a02 = k00 + shift * m00, k01 + shift * m01, k02 + shift * m02
    a11, a12, a22 = k11 + shift * m11, k12 + shift * m12, k22 + shift * m22
    l10, l20 = a01 / a00, a02 / a00
    e1 = a11 - l10 * a01
    e21 = a12 - l20 * a01
    l21 = e21 / e1
    e2 = a22 - l20 * a02 - l21 * e21
    b1 = m01 - l10 * m00
    b2 = m02 - l20 * m00 - l21 * b1
    c2 = b2 / e2
    c1 = b1 / e1 - l21 * c2
    c0 = m00 / a00 - l10 * c1 - l20 * c2
    square = c0 * (c0 * m00 + 2.0 * (c1 * m01 + c2 * m02)) + c1 * (c1 * m11 + 2.0 * c2 * m12) + c2 * c2 * m22
    scale = lax.rsqrt(square / params + EPSILON)
    c0, c1, c2 = c0 * scale, c1 * scale, c2 * scale

    def write(k, b):
        at = slice(b * LANE, (b + 1) * LANE)
        out_ref[:, pl.ds(pl.multiple_of(k * width + b * LANE, LANE), LANE)] = (
            c0 * base[k, :, at] + c1 * next1[k, :, at] + c2 * next2[k, :, at])

    whole = cols // width

    def write_piece(k, carry):
        for b in range(blocks):
            write(k, b)
        return carry
    lax.fori_loop(0, whole, write_piece, 0)
    for b in range((cols - whole * width) // LANE):
        write(whole, b)


def solution(mesh):
    nw, npar = mesh.shape["walk"], mesh.shape["param"]
    ny = Y_SIZE
    nz = npar // ny

    def body(jacobian, energies, shifts):
        cols = jacobian.shape[1]
        blocks = -(-(cols // LANE) // nw)
        width = blocks * LANE
        count = shifts.shape[0]
        f32 = jnp.float32
        return pl.pallas_call(
            functools.partial(kernel, (nw, ny, nz, cols, blocks)),
            out_shape=jax.ShapeDtypeStruct((count, cols), f32),
            in_specs=[
                pl.BlockSpec(memory_space=pl.ANY),
                pl.BlockSpec(memory_space=pl.ANY),
                pl.BlockSpec(memory_space=pl.ANY),
            ],
            out_specs=pl.BlockSpec(memory_space=pltpu.VMEM),
            scratch_shapes=[
                pltpu.VMEM((LANE, nw * width), f32),
                pltpu.VMEM((1, LANE), f32),
                pltpu.SMEM((count,), f32),
                pltpu.VMEM((nw, 1, 2 * width + LANE), f32),
                pltpu.VMEM((nw, 1, 2 * width + LANE), f32),
                pltpu.VMEM((nw, 1, 2 * width), f32),
                pltpu.VMEM((nw, 1, width), f32),
                pltpu.VMEM((nw, 1, width), f32),
                pltpu.VMEM((nw, 1, width), f32),
                pltpu.VMEM((2, nw, nw, 1, width), f32),
                pltpu.VMEM((3, nw, 1, LANE), f32),
                pltpu.VMEM((3, ny, 1, LANE), f32),
                pltpu.VMEM((3, nz, 1, LANE), f32),
                pltpu.VMEM((3, ny * nz, 1, LANE), f32),
                pltpu.SemaphoreType.DMA((nw + 2,)),
                pltpu.SemaphoreType.DMA((nw,)),
                pltpu.SemaphoreType.DMA((2, nw)),
                pltpu.SemaphoreType.DMA((2, nw)),
                pltpu.SemaphoreType.DMA((2, nw)),
                pltpu.SemaphoreType.DMA((3,)),
                pltpu.SemaphoreType.DMA((3,)),
                pltpu.SemaphoreType.DMA((3, 3)),
                pltpu.SemaphoreType.DMA((3, 3)),
                pltpu.SemaphoreType.REGULAR,
            ],
            compiler_params=pltpu.CompilerParams(
                collective_id=0, has_side_effects=True, vmem_limit_bytes=67043328
            ),
        )(jacobian, energies.reshape(1, -1), shifts)

    return jax.shard_map(
        body,
        mesh=mesh,
        in_specs=(P("walk", "param"), P("walk"), P()),
        out_specs=P(None, "param"),
        check_vma=False,
    )
```
